32 devices in a mesh: site: 8 (over y, x, core), scen: 4 (over z).
Axes of the slice: x: 2, y: 2, z: 4, core: 2. Of those that a mesh axis runs over, the one named last changes fastest.
Arguments:
- normals: bfloat16 [20480, 1344], P('site', 'scen'), may hold values from -6 to 6
- pattern: int32 [32, 40], replicated, may hold values from 0 to 79, as said below
- factor: bfloat16 [32, 40, 256, 256], P('site', None, 'scen'), may hold values from -0.0625 to 0.0625
- temporal: bfloat16 [168, 168], replicated, may hold values from -0.5 to 0.5
- capacity: float32 [8192], P('site'), may hold values from 0.05 to 0.4
- spread: float32 [8192], P('site'), may hold values from 0.2 to 0.8
- bus_map: int32 [8192], replicated, may hold values from 0 to 511
Outputs:
- bus_power: float32 [512, 1344], P('site', 'scen')
The draws below stay inside these ranges and needn't reach their ends.
Inputs may be any that keep to these rules, and one draw needn't show every extreme that they name: `pattern`: each block row names 40 different column blocks. The 4 block rows of one index of site (rows k * 4 to (k + 1) * 4 - 1) name at most 5 different column blocks among those held by any one index of site (blocks j * 10 to (j + 1) * 10 - 1), and exactly 5 among those held by index k itself.
All inputs are finite; a program needn't handle non-finite values.
Results may differ from the reference program's by a relative error of at most 0.0013.
Values may be sent and summed in bfloat16 or wider, within the bound.
A program may use at most 192 MiB of HBM per device.

```python
import math
import jax
import jax.numpy as jnp
from jax import lax

BLK = 256
HOURS = 168
NZ = 40
MAX_COLUMN_BLOCKS = 5
CB_DEV = 10
RB_DEV = 4
ROWS = 32
COLS = 80
SITES = 20480
SLAB = 8192
SCEN = 8
BUSES = 512


def candidate_slots(sub_key):
    return jax.random.permutation(sub_key, CB_DEV)[:MAX_COLUMN_BLOCKS].astype(jnp.int32)


def draw_pattern(key, part):
    owning_devices = ROWS // RB_DEV
    key_perm, pairing_key, key_hub, key_row = jax.random.split(jax.random.fold_in(key, 11), 4)
    local_slots = jax.vmap(candidate_slots)(jax.random.split(key_perm, owning_devices * owning_devices)).reshape(owning_devices, owning_devices, MAX_COLUMN_BLOCKS)
    holder = jnp.arange(owning_devices, dtype=jnp.int32)
    cand_columns = holder[None, :, None] * CB_DEV + local_slots
    raw_gap = jnp.abs(holder[:, None] - holder[None, :])
    block_separation = jnp.minimum(raw_gap, owning_devices - raw_gap)
    pairing_reward = jax.random.randint(pairing_key, (owning_devices, owning_devices), 0, 2048, dtype=jnp.int32) // (1 + block_separation)
    central_marker = jax.random.randint(key_hub, (owning_devices,), 0, 4, dtype=jnp.int32) == 0
    central_reward = jnp.where(central_marker, 1024, 0).astype(jnp.int32)
    ownership_reward = jnp.where(block_separation == 0, 100000, 0).astype(jnp.int32)
    device_reward = pairing_reward + central_reward[None, :] + ownership_reward
    row_holder_device = jnp.arange(ROWS, dtype=jnp.int32) // RB_DEV
    row_jitter = jax.random.randint(key_row, (ROWS, owning_devices, MAX_COLUMN_BLOCKS), 0, 1024, dtype=jnp.int32)
    tiebreak_jitter = jnp.arange(owning_devices * MAX_COLUMN_BLOCKS, dtype=jnp.int32).reshape(owning_devices, MAX_COLUMN_BLOCKS)
    placement_scores = (device_reward[row_holder_device][:, :, None] + row_jitter) * (owning_devices * MAX_COLUMN_BLOCKS) + tiebreak_jitter[None, :, :]
    chosen = lax.top_k(placement_scores.reshape(ROWS, owning_devices * MAX_COLUMN_BLOCKS), NZ)[1]
    row_cands = cand_columns[row_holder_device].reshape(ROWS, owning_devices * MAX_COLUMN_BLOCKS)
    return jnp.take_along_axis(row_cands, chosen, axis=1).astype(jnp.int32)


def touch_ends(result, stream_key, smallest, largest):
    index_at = [jax.random.randint(jax.random.fold_in(stream_key, axis), (), 0, length) for axis, length in enumerate(result.shape)]
    longest = result.shape.index(max(result.shape))
    next_to = index_at[:longest] + [(index_at[longest] + 1) % result.shape[longest]] + index_at[longest + 1:]
    return result.at[tuple(index_at)].set(smallest).at[tuple(next_to)].set(largest)


def level_of(stream_key, shape, cuts, least, high):
    gain, own = 1.0, jax.random.fold_in(stream_key, 6)
    for position, parts in cuts:
        draws = jnp.exp(jax.random.uniform(jax.random.fold_in(own, position), (parts,), jnp.float32, least / len(cuts), high / len(cuts)))
        gain = gain * jnp.repeat(draws, shape[position] // parts).reshape([-1 if axis == position else 1 for axis in range(len(shape))])
    return gain


def gaussian(own_key, dims, scale, bound, cuts=(), kind=jnp.bfloat16):
    result = scale * jax.random.normal(own_key, dims, jnp.float32)
    if cuts:
        result = result * level_of(own_key, dims, cuts, -0.22, 0.18)
    return jnp.clip(result, -bound, bound).astype(kind)


def setup_inputs(seed: int = 0) -> dict:
    splits = jax.random.split(jax.random.key(seed), 8)
    return {
        "normals": gaussian(splits[0], (SITES, SCEN * HOURS), 1.0, 6.0, ((0, 8), (1, 4))),
        "pattern": draw_pattern(jax.random.fold_in(splits[7], 71), 0),
        "factor": gaussian(splits[2], (ROWS, NZ, BLK, BLK), (NZ * BLK) ** -0.5, 0.0625, ((0, 8), (2, 4))),
        "temporal": gaussian(splits[3], (HOURS, HOURS), HOURS ** -0.5, 0.5),
        "capacity": jnp.clip(jnp.exp(math.log(0.4) - 2.0794415 * jax.random.uniform(splits[4], (SLAB,), jnp.float32) ** level_of(splits[4], (SLAB,), ((0, 8),), -0.2, 0.2)), 0.05, 0.4),
        "spread": jnp.clip(jnp.exp(math.log(0.8) - 1.3862944 * jax.random.uniform(splits[5], (SLAB,), jnp.float32) ** level_of(splits[5], (SLAB,), ((0, 8),), -0.2, 0.2)), 0.2, 0.8),
        "bus_map": touch_ends(jax.random.randint(splits[6], (SLAB,), 0, BUSES), jax.random.fold_in(splits[6], 1), 0, BUSES - 1).astype(jnp.int32),
    }


def reference(normals, pattern, factor, temporal, capacity, spread, bus_map):
    row_width = SCEN * HOURS
    blocks = normals.reshape(COLS, BLK, row_width)

    def one_block_row(inputs):
        columns, factor_row = inputs
        picked = jnp.take(blocks, columns.astype(jnp.int32), axis=0)
        spatial = jnp.einsum("tij,tjw->iw", factor_row.astype(jnp.float32), picked.astype(jnp.float32))
        return spatial.astype(jnp.bfloat16)

    spatial = lax.map(one_block_row, (pattern, factor))
    hourly = spatial.reshape(SLAB, SCEN, HOURS).astype(jnp.float32)
    weather = jnp.einsum("nsg,hg->nsh", hourly, temporal.astype(jnp.float32))
    scale_rows = capacity[:, None, None]
    spread_rows = spread[:, None, None]
    injected = (scale_rows * jnp.exp(spread_rows * weather - 0.5 * spread_rows * spread_rows)).astype(jnp.bfloat16)
    injected = injected.reshape(SLAB, row_width).astype(jnp.float32)
    return jax.ops.segment_sum(injected, bus_map.astype(jnp.int32), num_segments=BUSES)
```

```python
import functools

import jax
import jax.numpy as jnp
from jax import lax
from jax.experimental import pallas as pl
from jax.experimental.pallas import tpu as pltpu
from jax.sharding import PartitionSpec as P

MAX_COLUMN_BLOCKS = 5
PAIR = 2
CHUNKS = 3
LANES = 128
VMEM_LIMIT = 67043328
MESH = pl.DeviceIdType.MESH


def kernel(
    chips,
    groups,
    slots,
    hours,
    pattern_ref,
    z_ref,
    f_ref,
    temporal_ref,
    capacity_ref,
    spreads_ref,
    buses_ref,
    out_ref,
    z_all,
    z_work,
    f_raw,
    f_sorted,
    f_all,
    s_send,
    s_own,
    s_all,
    s_sum,
    b_send,
    b_all,
    x_send,
    x_all,
    c_send,
    c_all,
    onehot,
    scale_ref,
    spread_ref,
    pos,
    need,
    ranks,
    gathered,
    tables,
    scalars,
    local_sem,
    zsend,
    zrecv,
    psend,
    precv,
    fsend,
    frecv,
    ssend,
    srecv,
    bsend,
    brecv,
    csend,
    crecv,
    xsend,
    xrecv,
):
    k = lax.axis_index("site")
    z = lax.axis_index("scen")
    q = k // PAIR
    c = k % PAIR
    other = q * PAIR + (PAIR - 1 - c)
    rows_here, nz, height, blk = f_ref.shape
    width, depth = z_ref.shape
    bounds = bounds_of(width)
    each = slots // chips
    scens = width // hours
    shared = b_send.shape[3]
    sites = chips * PAIR
    held = depth // blk
    lanes = pos.shape[1]
    rows = rows_here * height
    last = groups - 1

    z_load = pltpu.make_async_copy(z_ref, z_all.at[z, c], local_sem.at[0])
    z_load.start()
    f_load = pltpu.make_async_copy(f_ref, f_raw, local_sem.at[1])
    f_load.start()

    barrier = pltpu.get_barrier_semaphore()

    def peer(e):
        return (q + e) % chips

    for d in range(1, groups):
        pl.semaphore_signal(barrier, inc=1, device_id=(k, (z + d) % groups), device_id_type=MESH)
    for e in range(1, chips):
        pl.semaphore_signal(barrier, inc=1, device_id=(peer(e) * PAIR + c, z), device_id_type=MESH)
    pl.semaphore_signal(barrier, inc=1, device_id=(other, z), device_id_type=MESH)

    lane = lax.broadcasted_iota(jnp.int32, (1, lanes), 1)
    owner = jnp.zeros_like(lane)
    for j in range(1, sites):
        owner = owner + jnp.where(lane >= j * held, 1, 0)
    local = lane - owner * held
    found = jnp.zeros(pos.shape, jnp.int32)
    for t in range(nz):
        found = jnp.where(pattern_ref[:, t : t + 1] == lane, t + 1, found)
    pos[...] = found
    for i in range(sites):
        line = pos[i * rows_here : i * rows_here + 1, :]
        for r in range(1, rows_here):
            at = i * rows_here + r
            line = jnp.maximum(line, pos[at : at + 1, :])
        need[i : i + 1, :] = jnp.where(line > 0, 1, 0)
    wanted = need[...]
    before = jnp.zeros_like(wanted)
    for d in range(1, held):
        before = before + jnp.where(local >= d, pltpu.roll(wanted, d, 1), 0)
    ranks[...] = before

    half_rows = tables.shape[0] // 2
    column = lax.broadcasted_iota(jnp.int32, (half_rows, tables.shape[1]), 1)
    gathered[...] = jnp.zeros_like(gathered)
    for r in range(rows_here):
        gathered[0, r : r + 1, :] = pos[pl.ds(k * rows_here + r, 1), :]
    for i in range(chips):
        gathered[1, i : i + 1, :] = need[pl.ds(i * PAIR + c, 1), :]
        gathered[2, i : i + 1, :] = ranks[pl.ds(i * PAIR + c, 1), :]
    own_slot = owner * MAX_COLUMN_BLOCKS + ranks[pl.ds(k, 1), :]
    own_slot = jnp.where(need[pl.ds(k, 1), :] > 0, own_slot, -1)
    places = jnp.zeros(column.shape, jnp.int32)
    positions = gathered[0]
    for t in range(slots):
        at = jnp.sum(jnp.where(own_slot == t, positions, 0), axis=1, keepdims=True)
        places = jnp.where(column == t, at, places)
    tables[0:half_rows, :] = places - 1
    blocks = jnp.zeros(column.shape, jnp.int32)
    needs, orders = gathered[1], gathered[2]
    first = q * PAIR * held
    for half in range(PAIR):
        mine = jnp.where(owner == q * PAIR + half, needs, 0)
        for j in range(MAX_COLUMN_BLOCKS):
            hit = jnp.where(orders == j, mine, 0)
            at = jnp.sum(hit * (lane - first), axis=1, keepdims=True)
            blocks = jnp.where(column == half * MAX_COLUMN_BLOCKS + j, at, blocks)
    tables[half_rows:, :] = blocks
    t_load = pltpu.make_async_copy(tables, scalars, local_sem.at[2])
    t_load.start()

    narrow = capacity_ref.shape[1]
    narrow_lane = lax.broadcasted_iota(jnp.int32, (8, narrow), 1)
    offset = z * height

    def rows_of(ref, base):
        parts = []
        for start in range(0, rows, narrow):
            part = None
            for r in range(start // height, min((start + narrow) // height, rows_here)):
                line = ref[pl.ds(base + r * blk // narrow + offset // narrow, 1), :]
                line = jnp.broadcast_to(line, narrow_lane.shape)
                shift = (r * height - start + narrow - offset % narrow) % narrow
                line = pltpu.roll(line, shift, 1)
                if part is None:
                    part = line
                else:
                    part = jnp.where(narrow_lane >= r * height - start, line, part)
            parts.append(part[0:1])
        return jnp.concatenate(parts, axis=1) if len(parts) > 1 else parts[0]

    scale_ref[...] = rows_of(capacity_ref, 0)
    spread_ref[...] = rows_of(spreads_ref, 0)
    maps = rows_of(buses_ref, k * (rows_here * blk // narrow))
    bus_ids = lax.broadcasted_iota(jnp.int32, onehot.shape, 0)
    onehot[...] = jnp.where(bus_ids == maps, 1.0, 0.0).astype(onehot.dtype)
    t_load.wait()
    pl.semaphore_wait(barrier, groups - 1 + chips - 1 + 1)

    def piece(ch):
        return pl.ds(bounds[ch], bounds[ch + 1] - bounds[ch])

    def hop(g, ch, up, source=None):
        part = z_all.at[g, c, piece(ch)]
        return pltpu.make_async_remote_copy(
            src_ref=part if source is None else source,
            dst_ref=part,
            send_sem=zsend.at[up, g, ch],
            recv_sem=zrecv.at[g, ch],
            device_id=(k, z + 1 if up else z - 1),
            device_id_type=MESH,
        )

    def share(g, ch, source=None):
        part = z_all.at[g, c, piece(ch)]
        return pltpu.make_async_remote_copy(
            src_ref=part if source is None else source,
            dst_ref=part,
            send_sem=psend.at[g, ch],
            recv_sem=precv.at[g, ch],
            device_id=(other, z),
            device_id_type=MESH,
        )

    def came_in(g, ch):
        part = z_all.at[g, c, piece(ch)]
        return pltpu.make_async_remote_copy(
            src_ref=part,
            dst_ref=part,
            send_sem=psend.at[g, ch],
            recv_sem=zrecv.at[g, ch],
            device_id=(other, z),
            device_id_type=MESH,
        )

    def shared_in(g, ch):
        part = z_all.at[g, 1 - c, piece(ch)]
        return pltpu.make_async_remote_copy(
            src_ref=part,
            dst_ref=part,
            send_sem=psend.at[g, ch],
            recv_sem=precv.at[g, ch],
            device_id=(other, z),
            device_id_type=MESH,
        )

    for ch in range(CHUNKS):
        own = z_ref.at[piece(ch)]

        @pl.when(z < last)
        def _():
            hop(z, ch, 1, own).start()

        @pl.when(z > 0)
        def _():
            hop(z, ch, 0, own).start()

    for ch in range(CHUNKS):
        share(z, ch, z_ref.at[piece(ch)]).start()

    def relay(g, ch):
        came_in(g, ch).wait_recv()

        @pl.when(jnp.logical_and(g < z, z < last))
        def _():
            hop(g, ch, 1).start()

        @pl.when(jnp.logical_and(g > z, z > 0))
        def _():
            hop(g, ch, 0).start()

        share(g, ch).start()

    def arrivals(d, ch):
        @pl.when(z - d >= 0)
        def _():
            relay(z - d, ch)

        @pl.when(z + d <= last)
        def _():
            relay(z + d, ch)

    def f_copy(target, source):
        return pltpu.make_async_remote_copy(
            src_ref=f_sorted.at[target],
            dst_ref=f_all.at[source],
            send_sem=fsend.at[target],
            recv_sem=frecv.at[source],
            device_id=(target * PAIR + c, z),
            device_id_type=MESH,
        )

    f_load.wait()

    def sort_for(target, store):
        def one(s, carry):
            for r in range(rows_here):
                t = scalars[r, target * each + s]
                block = f_raw[r, jnp.maximum(t, 0)]
                if slots > nz:
                    block = jnp.where(t >= 0, block, jnp.zeros_like(block))
                store(s, r, block)
            return carry

        lax.fori_loop(0, each, one, 0)

    for e in range(1, chips):
        target = peer(e)

        def to_send(s, r, block):
            f_sorted[target, s, pl.ds(r * height, height), :] = block

        sort_for(target, to_send)
        f_copy(target, q).start()

    def to_own(s, r, block):
        f_all[q, s, pl.ds(r * height, height), :] = block

    sort_for(q, to_own)

    z_load.wait()

    for ch in range(CHUNKS):
        arrivals(1, ch)
    if groups > 2:
        arrivals(2, 0)
    for e in range(1, chips):
        f_copy(q, peer(e)).wait_recv()

    fewer = jnp.minimum(z, last - z)
    more = jnp.where(z < last - z, 1, -1)

    def group_at(p):
        near = jnp.where(p % 2 == 1, -((p + 1) // 2), (p + 1) // 2)
        far = more * (p - fewer)
        return z + jnp.where(p <= 2 * fewer, near, far)

    def s_copy(g, ch, slot, target, source):
        size = bounds[ch + 1] - bounds[ch]
        return pltpu.make_async_remote_copy(
            src_ref=s_send.at[slot, target, pl.ds(0, size)],
            dst_ref=s_all.at[g, ch, source, pl.ds(0, size)],
            send_sem=ssend.at[slot, target],
            recv_sem=srecv.at[g, ch, source],
            device_id=(target * PAIR + c, z),
            device_id_type=MESH,
        )

    def b_copy(g, s, target, source):
        return pltpu.make_async_remote_copy(
            src_ref=b_send.at[s, target],
            dst_ref=b_all.at[g, s, source],
            send_sem=bsend.at[s, target],
            recv_sem=brecv.at[g, s, source],
            device_id=(target * PAIR + c, z),
            device_id_type=MESH,
        )

    def x_copy(g):
        return pltpu.make_async_remote_copy(
            src_ref=x_send.at[g],
            dst_ref=x_all.at[g],
            send_sem=xsend.at[g],
            recv_sem=xrecv.at[g],
            device_id=(other, z),
            device_id_type=MESH,
        )

    def c_copy(g, source):
        return pltpu.make_async_remote_copy(
            src_ref=c_send.at[g],
            dst_ref=c_all.at[source],
            send_sem=csend.at[g],
            recv_sem=crecv.at[source],
            device_id=(k, g),
            device_id_type=MESH,
        )

    def multiply(g, ch, slot):
        size = bounds[ch + 1] - bounds[ch]
        shared_in(g, ch).wait_recv()
        for half in range(PAIR):
            for b in range(held):
                z_work[half * held + b, 0:size, :] = z_all[
                    g, half, piece(ch), b * blk : (b + 1) * blk
                ]

        def product(i):
            total = None
            for s in range(each):
                term = lax.dot_general(
                    z_work[scalars[half_rows + i, s], 0:size, :],
                    f_all[i, s],
                    (((1,), (1,)), ((), ())),
                    preferred_element_type=jnp.float32,
                )
                total = term if total is None else total + term
            return total

        def one(e, carry):
            target = peer(e)
            s_send[slot, target, 0:size, :] = product(target).astype(s_send.dtype)
            s_copy(g, ch, slot, target, q).start()
            return carry

        lax.fori_loop(1, chips, one, 0)
        s_own[slot, 0:size, :] = product(q)

    def finish(p, ch):
        g = group_at(p)
        size = bounds[ch + 1] - bounds[ch]
        total = s_own[(p * CHUNKS + ch) % 2, 0:size, :]
        for e in range(1, chips):
            s_copy(g, ch, 0, q, peer(e)).wait_recv()
            total = total + s_all[g, ch, peer(e), 0:size, :].astype(jnp.float32)
        s_sum[bounds[ch] : bounds[ch + 1], :] = total
        for s in range(scens):
            if not bounds[ch] < (s + 1) * hours <= bounds[ch + 1]:
                continue
            spatial = s_sum[s * hours : (s + 1) * hours, :].astype(jnp.bfloat16)
            weather = jnp.dot(temporal_ref[...], spatial, preferred_element_type=jnp.float32)
            spread = spread_ref[...]
            values = scale_ref[...] * jnp.exp(spread * weather - 0.5 * spread * spread)
            sums = lax.dot_general(
                values.astype(jnp.bfloat16),
                onehot[...],
                (((1,), (1,)), ((), ())),
                preferred_element_type=jnp.float32,
            ).astype(b_send.dtype)

            @pl.when(p > 0)
            def _():
                for e in range(1, chips):
                    b_copy(g, s, peer(e), q).wait_send()

            for i in range(chips):
                b_send[s, i] = sums[:, i * shared : (i + 1) * shared]
            for e in range(1, chips):
                b_copy(g, s, peer(e), q).start()
            b_all[g, s, q] = b_send[s, q]

    def exchange(p):
        g = group_at(p)
        parts = []
        for s in range(scens):
            for e in range(1, chips):
                b_copy(g, s, q, peer(e)).wait_recv()
            total = b_all[g, s, 0].astype(jnp.float32)
            for i in range(1, chips):
                total = total + b_all[g, s, i].astype(jnp.float32)
            parts.append(total)
        side = lax.broadcasted_iota(jnp.int32, parts[0].shape, 1) // (shared // PAIR)
        packed = []
        for core in range(PAIR):
            total = None
            for s in range(scens):
                shift = ((s - core) * (shared // PAIR)) % shared
                part = pltpu.roll(parts[s], shift, 1) if shift else parts[s]
                total = part if total is None else jnp.where(side == s, part, total)
            packed.append(total)
        x_send[g] = jnp.where(c == 0, packed[1], packed[0])
        x_copy(g).start()
        c_send[g] = jnp.where(c == 0, packed[0], packed[1])

    def forward(p):
        g = group_at(p)
        x_copy(g).wait_recv()
        total = c_send[g] + x_all[g]

        @pl.when(p == 0)
        def _():
            c_all[z] = total

        @pl.when(p > 0)
        def _():
            c_send[g] = total
            c_copy(g, z).start()

    def free(g, ch, slot):
        for e in range(1, chips):
            s_copy(g, ch, slot, peer(e), q).wait_send()

    def position(p, carry):
        g = group_at(p)
        for ch in range(CHUNKS):
            slot = (p * CHUNKS + ch) % 2
            if ch >= 2:
                free(g, ch - 2, slot)
            else:

                @pl.when(p > 0)
                def _():
                    free(g, ch + CHUNKS - 2, slot)

            multiply(g, ch, slot)
            if ch > 0:
                finish(p, ch - 1)

                @pl.when(p > 0)
                def _():
                    exchange(p - 1) if ch == 1 else forward(p - 1)

            else:

                @pl.when(p > 0)
                def _():
                    finish(p - 1, CHUNKS - 1)

            if ch + 1 < CHUNKS:

                @pl.when(p >= 2)
                def _():
                    arrivals(p, ch + 1)
            else:

                @pl.when(jnp.logical_and(p >= 2, p < last))
                def _():
                    arrivals(p + 1, 0)

        return carry

    lax.fori_loop(0, groups, position, 0)
    finish(last, CHUNKS - 1)
    exchange(last)
    forward(last)

    free(z, CHUNKS - 2, (groups * CHUNKS - 2) % 2)
    free(z, CHUNKS - 1, (groups * CHUNKS - 1) % 2)
    for e in range(1, chips):
        f_copy(peer(e), q).wait_send()
        for s in range(scens):
            b_copy(z, s, peer(e), q).wait_send()
    for g in range(groups):
        x_copy(g).wait_send()
        for ch in range(CHUNKS):
            share(g, ch).wait_send()

            @pl.when(jnp.logical_and(g <= z, z < last))
            def _():
                hop(g, ch, 1).wait_send()

            @pl.when(jnp.logical_and(g >= z, z > 0))
            def _():
                hop(g, ch, 0).wait_send()

    total = c_all[z]
    for d in range(1, groups):
        source = (z + d) % groups
        c_copy(z, source).wait_recv()
        total = total + c_all[source]
    turned = total.T
    share_of = shared // PAIR
    for s in range(scens):
        out_ref[:, s * hours : (s + 1) * hours] = turned[s * share_of : (s + 1) * share_of]
    for d in range(1, groups):
        c_copy((z + d) % groups, z).wait_send()


def bounds_of(width):
    small = width // 7
    large = (width - small) // (CHUNKS - 1)
    return [large * i for i in range(CHUNKS)] + [width]


def shards(normals, pattern, factor, temporal, capacity, spread, bus_map, buses):
    sites = lax.axis_size("site")
    groups = lax.axis_size("scen")
    depth, width = normals.shape
    rows_here, nz, height, blk = factor.shape
    hours = temporal.shape[0]
    scens = width // hours
    chips = sites // PAIR
    bounds = bounds_of(width)
    step = max(b - a for a, b in zip(bounds, bounds[1:]))
    slots = sites * MAX_COLUMN_BLOCKS
    each = slots // chips
    rows = rows_here * height
    shared = buses // chips
    block_count = depth // blk
    lanes = -(-block_count * sites // LANES) * LANES
    half_rows = -(-max(chips, rows_here) // 8) * 8

    bf16, f32, i32 = jnp.bfloat16, jnp.float32, jnp.int32
    dma = pltpu.SemaphoreType.DMA
    whole = pl.BlockSpec(memory_space=pltpu.VMEM)
    anywhere = pl.BlockSpec(memory_space=pl.ANY)
    return pl.pallas_call(
        functools.partial(kernel, chips, groups, slots, hours),
        out_shape=jax.ShapeDtypeStruct((buses // sites, width), f32),
        in_specs=[whole, anywhere, anywhere, whole, whole, whole, whole],
        out_specs=whole,
        scratch_shapes=[
            pltpu.VMEM((groups, PAIR, width, depth), bf16),
            pltpu.VMEM((PAIR * block_count, step, blk), bf16),
            pltpu.VMEM((rows_here, nz, height, blk), bf16),
            pltpu.VMEM((chips, each, rows, blk), bf16),
            pltpu.VMEM((chips, each, rows, blk), bf16),
            pltpu.VMEM((2, chips, step, rows), bf16),
            pltpu.VMEM((2, step, rows), f32),
            pltpu.VMEM((groups, CHUNKS, chips, step, rows), bf16),
            pltpu.VMEM((width, rows), f32),
            pltpu.VMEM((scens, chips, hours, shared), bf16),
            pltpu.VMEM((groups, scens, chips, hours, shared), bf16),
            pltpu.VMEM((groups, hours, shared), f32),
            pltpu.VMEM((groups, hours, shared), f32),
            pltpu.VMEM((groups, hours, shared), f32),
            pltpu.VMEM((groups, hours, shared), f32),
            pltpu.VMEM((buses, rows), bf16),
            pltpu.VMEM((1, rows), f32),
            pltpu.VMEM((1, rows), f32),
            pltpu.VMEM((pattern.shape[0], lanes), i32),
            pltpu.VMEM((sites, lanes), i32),
            pltpu.VMEM((sites, lanes), i32),
            pltpu.VMEM((3, half_rows, lanes), i32),
            pltpu.VMEM((2 * half_rows, LANES), i32),
            pltpu.SMEM((2 * half_rows, LANES), i32),
            dma((3,)),
            dma((2, groups, CHUNKS)),
            dma((groups, CHUNKS)),
            dma((groups, CHUNKS)),
            dma((groups, CHUNKS)),
            dma((chips,)),
            dma((chips,)),
            dma((2, chips)),
            dma((groups, CHUNKS, chips)),
            dma((scens, chips)),
            dma((groups, scens, chips)),
            dma((groups,)),
            dma((groups,)),
            dma((groups,)),
            dma((groups,)),
        ],
        compiler_params=pltpu.CompilerParams(
            collective_id=0, has_side_effects=True, vmem_limit_bytes=VMEM_LIMIT
        ),
    )(
        pattern,
        normals.T,
        factor,
        temporal,
        capacity.reshape(-1, LANES),
        spread.reshape(-1, LANES),
        bus_map.reshape(-1, LANES),
    )


def solution(mesh):
    placed = (P("site", "scen"), P(), P("site", None, "scen", None), P(), P("site"), P("site"), P())
    sites = mesh.shape["site"]

    def whole(normals, pattern, factor, temporal, capacity, spread, bus_map):
        buses = factor.shape[0] * factor.shape[3] // 16

        def body(*args):
            return shards(*args, buses)

        return jax.shard_map(
            body, mesh=mesh, in_specs=placed, out_specs=P("site", "scen"), check_vma=False
        )(normals, pattern, factor, temporal, capacity, spread, bus_map)

    return whole
```

```python
import functools

import jax
import jax.numpy as jnp
from jax import lax
from jax.experimental import pallas as pl
from jax.experimental.pallas import tpu as pltpu
from jax.sharding import PartitionSpec as P

MAX_COLUMN_BLOCKS = 5
PAIR = 2
CHUNKS = 3
LANES = 128
VMEM_LIMIT = 67043328
MESH = pl.DeviceIdType.MESH


def kernel(
    chips,
    groups,
    slots,
    hours,
    pattern_hbm,
    z_ref,
    f_ref,
    temporal_hbm,
    capacity_hbm,
    spreads_hbm,
    buses_hbm,
    near_ref,
    far_ref,
    pattern_ref,
    temporal_ref,
    capacity_ref,
    spreads_ref,
    buses_ref,
    z_all,
    z_work,
    f_raw,
    f_sorted,
    f_all,
    s_send,
    s_own,
    s_all,
    s_sum,
    b_send,
    b_all,
    c_send,
    c_all,
    c_mid,
    c_sum,
    onehot,
    scale_ref,
    spread_ref,
    pos,
    need,
    ranks,
    gathered,
    tables,
    scalars,
    local_sem,
    zsend,
    zrecv,
    psend,
    precv,
    fsend,
    frecv,
    ssend,
    srecv,
    bsend,
    brecv,
    csend,
    crecv,
    mrecv,
    meet,
):
    k = lax.axis_index("site")
    z = lax.axis_index("scen")
    q = k // PAIR
    c = k % PAIR
    other = q * PAIR + (PAIR - 1 - c)
    rows_here, nz, height, blk = f_ref.shape
    width, depth = z_ref.shape
    bounds = bounds_of(width)
    each = slots // chips
    scens = width // hours
    share_of = near_ref.shape[0]
    shared = share_of * PAIR
    packed_rows = b_send.shape[2]
    sites = chips * PAIR
    held = depth // blk
    lanes = pos.shape[1]
    rows = rows_here * height
    last = groups - 1

    bits = [1 << i for i in range(chips.bit_length() - 1)]

    def across(bit):
        return q + bit - 2 * bit * ((q // bit) % 2)

    barrier = pltpu.get_barrier_semaphore()

    def peer(e):
        return (q + e) % chips

    def greet(device):
        pl.semaphore_signal(barrier, inc=1, device_id=device, device_id_type=MESH)

    @pl.when(z < last)
    def _():
        greet((k, z + 1))

    @pl.when(z > 0)
    def _():
        greet((k, z - 1))

    greet((other, z))
    for bit in bits:
        greet((across(bit) * PAIR + c, z))

    small = [
        (pattern_hbm, pattern_ref),
        (temporal_hbm, temporal_ref),
        (capacity_hbm, capacity_ref),
        (spreads_hbm, spreads_ref),
        (buses_hbm, buses_ref),
    ]
    loads = [
        pltpu.make_async_copy(source, target, local_sem.at[3 + i])
        for i, (source, target) in enumerate(small)
    ]
    for load in loads:
        load.start()
    ends = jnp.where(z < last, 1, 0) + jnp.where(z > 0, 1, 0)
    pl.semaphore_wait(barrier, 1 + len(bits) + ends)

    def piece(ch):
        return pl.ds(bounds[ch], bounds[ch + 1] - bounds[ch])

    def hop(g, ch, up, source=None):
        part = z_all.at[g, c, piece(ch)]
        return pltpu.make_async_remote_copy(
            src_ref=part if source is None else source,
            dst_ref=part,
            send_sem=zsend.at[up, g, ch],
            recv_sem=zrecv.at[g, ch],
            device_id=(k, z + 1 if up else z - 1),
            device_id_type=MESH,
        )

    def share(g, ch, source=None):
        part = z_all.at[g, c, piece(ch)]
        return pltpu.make_async_remote_copy(
            src_ref=part if source is None else source,
            dst_ref=part,
            send_sem=psend.at[g, ch],
            recv_sem=precv.at[g, ch],
            device_id=(other, z),
            device_id_type=MESH,
        )

    def came_in(g, ch):
        part = z_all.at[g, c, piece(ch)]
        return pltpu.make_async_remote_copy(
            src_ref=part,
            dst_ref=part,
            send_sem=psend.at[g, ch],
            recv_sem=zrecv.at[g, ch],
            device_id=(other, z),
            device_id_type=MESH,
        )

    def shared_in(g, ch):
        part = z_all.at[g, 1 - c, piece(ch)]
        return pltpu.make_async_remote_copy(
            src_ref=part,
            dst_ref=part,
            send_sem=psend.at[g, ch],
            recv_sem=precv.at[g, ch],
            device_id=(other, z),
            device_id_type=MESH,
        )

    for ch in range(CHUNKS):
        own = z_ref.at[piece(ch)]

        @pl.when(z < last)
        def _():
            hop(z, ch, 1, own).start()

        @pl.when(z > 0)
        def _():
            hop(z, ch, 0, own).start()

    for ch in range(CHUNKS):
        share(z, ch, z_ref.at[piece(ch)]).start()

    for i, bit in enumerate(bits[:-1]):
        pl.semaphore_signal(
            meet.at[i], inc=1, device_id=(across(bit) * PAIR + c, z), device_id_type=MESH
        )
        pl.semaphore_wait(meet.at[i], 1)

    z_load = pltpu.make_async_copy(z_ref, z_all.at[z, c], local_sem.at[0])
    z_load.start()
    f_load = pltpu.make_async_copy(f_ref, f_raw, local_sem.at[1])
    f_load.start()
    for load in loads:
        load.wait()

    lane = lax.broadcasted_iota(jnp.int32, (1, lanes), 1)
    owner = jnp.zeros_like(lane)
    for j in range(1, sites):
        owner = owner + jnp.where(lane >= j * held, 1, 0)
    local = lane - owner * held
    found = jnp.zeros(pos.shape, jnp.int32)
    for t in range(nz):
        found = jnp.where(pattern_ref[:, t : t + 1] == lane, t + 1, found)
    pos[...] = found
    for i in range(sites):
        line = pos[i * rows_here : i * rows_here + 1, :]
        for r in range(1, rows_here):
            at = i * rows_here + r
            line = jnp.maximum(line, pos[at : at + 1, :])
        need[i : i + 1, :] = jnp.where(line > 0, 1, 0)
    wanted = need[...]
    before = jnp.zeros_like(wanted)
    for d in range(1, held):
        before = before + jnp.where(local >= d, pltpu.roll(wanted, d, 1), 0)
    ranks[...] = before

    half_rows = tables.shape[0] // 2
    column = lax.broadcasted_iota(jnp.int32, (half_rows, tables.shape[1]), 1)
    gathered[...] = jnp.zeros_like(gathered)
    for r in range(rows_here):
        gathered[0, r : r + 1, :] = pos[pl.ds(k * rows_here + r, 1), :]
    for i in range(chips):
        gathered[1, i : i + 1, :] = need[pl.ds(i * PAIR + c, 1), :]
        gathered[2, i : i + 1, :] = ranks[pl.ds(i * PAIR + c, 1), :]
    own_slot = owner * MAX_COLUMN_BLOCKS + ranks[pl.ds(k, 1), :]
    own_slot = jnp.where(need[pl.ds(k, 1), :] > 0, own_slot, -1)
    places = jnp.zeros(column.shape, jnp.int32)
    positions = gathered[0]
    for t in range(slots):
        at = jnp.sum(jnp.where(own_slot == t, positions, 0), axis=1, keepdims=True)
        places = jnp.where(column == t, at, places)
    tables[0:half_rows, :] = places - 1
    blocks = jnp.zeros(column.shape, jnp.int32)
    needs, orders = gathered[1], gathered[2]
    first = q * PAIR * held
    for half in range(PAIR):
        mine = jnp.where(owner == q * PAIR + half, needs, 0)
        for j in range(MAX_COLUMN_BLOCKS):
            hit = jnp.where(orders == j, mine, 0)
            at = jnp.sum(hit * (lane - first), axis=1, keepdims=True)
            blocks = jnp.where(column == half * MAX_COLUMN_BLOCKS + j, at, blocks)
    tables[half_rows:, :] = blocks
    t_load = pltpu.make_async_copy(tables, scalars, local_sem.at[2])
    t_load.start()

    narrow = capacity_ref.shape[1]
    narrow_lane = lax.broadcasted_iota(jnp.int32, (8, narrow), 1)
    offset = z * height

    def rows_of(ref, base):
        parts = []
        for start in range(0, rows, narrow):
            part = None
            for r in range(start // height, min((start + narrow) // height, rows_here)):
                line = ref[pl.ds(base + r * blk // narrow + offset // narrow, 1), :]
                line = jnp.broadcast_to(line, narrow_lane.shape)
                shift = (r * height - start + narrow - offset % narrow) % narrow
                line = pltpu.roll(line, shift, 1)
                if part is None:
                    part = line
                else:
                    part = jnp.where(narrow_lane >= r * height - start, line, part)
            parts.append(part[0:1])
        return jnp.concatenate(parts, axis=1) if len(parts) > 1 else parts[0]

    scale_ref[...] = rows_of(capacity_ref, 0)
    spread_ref[...] = rows_of(spreads_ref, 0)
    maps = rows_of(buses_ref, k * (rows_here * blk // narrow))
    bus_ids = lax.broadcasted_iota(jnp.int32, onehot.shape, 0)
    onehot[...] = jnp.where(bus_ids == maps, 1.0, 0.0).astype(onehot.dtype)
    t_load.wait()

    def relay(g, ch):
        came_in(g, ch).wait_recv()

        @pl.when(jnp.logical_and(g < z, z < last))
        def _():
            hop(g, ch, 1).start()

        @pl.when(jnp.logical_and(g > z, z > 0))
        def _():
            hop(g, ch, 0).start()

        share(g, ch).start()

    def arrivals(d, ch):
        @pl.when(z - d >= 0)
        def _():
            relay(z - d, ch)

        @pl.when(z + d <= last)
        def _():
            relay(z + d, ch)

    def f_copy(target, source):
        return pltpu.make_async_remote_copy(
            src_ref=f_sorted.at[target],
            dst_ref=f_all.at[source],
            send_sem=fsend.at[target],
            recv_sem=frecv.at[source],
            device_id=(target * PAIR + c, z),
            device_id_type=MESH,
        )

    f_load.wait()

    def sort_for(target, store):
        def one(s, carry):
            blocks = []
            for r in range(rows_here):
                t = scalars[r, target * each + s]
                block = f_raw[r, jnp.maximum(t, 0)]
                if slots > nz:
                    block = jnp.where(t >= 0, block, jnp.zeros_like(block))
                blocks.append(block)
            store(s, jnp.concatenate(blocks, axis=0).T)
            return carry

        lax.fori_loop(0, each, one, 0)

    for e in range(1, chips):
        target = peer(e)

        def to_send(s, tile):
            f_sorted[target, s] = tile

        sort_for(target, to_send)
        f_copy(target, q).start()

    def to_own(s, tile):
        f_all[q, s] = tile

    sort_for(q, to_own)

    z_load.wait()

    for ch in range(CHUNKS):
        arrivals(1, ch)
    if groups > 2:
        arrivals(2, 0)
    for e in range(1, chips):
        f_copy(q, peer(e)).wait_recv()

    fewer = jnp.minimum(z, last - z)
    more = jnp.where(z < last - z, 1, -1)

    def group_at(p):
        near = jnp.where(p % 2 == 1, -((p + 1) // 2), (p + 1) // 2)
        far = more * (p - fewer)
        return z + jnp.where(p <= 2 * fewer, near, far)

    def s_copy(g, ch, slot, target, source):
        size = bounds[ch + 1] - bounds[ch]
        return pltpu.make_async_remote_copy(
            src_ref=s_send.at[slot, target, pl.ds(0, size)],
            dst_ref=s_all.at[g, ch, source, pl.ds(0, size)],
            send_sem=ssend.at[slot, target],
            recv_sem=srecv.at[g, ch, source],
            device_id=(target * PAIR + c, z),
            device_id_type=MESH,
        )

    def b_copy(g, s, target, source):
        return pltpu.make_async_remote_copy(
            src_ref=b_send.at[s, target],
            dst_ref=b_all.at[g, s, source],
            send_sem=bsend.at[s, target],
            recv_sem=brecv.at[g, s, source],
            device_id=(target, z),
            device_id_type=MESH,
        )

    def seat(e):
        return (k + e) % sites

    def c_copy(g, s, source):
        return pltpu.make_async_remote_copy(
            src_ref=c_send.at[g, s],
            dst_ref=c_all.at[s, source],
            send_sem=csend.at[g, s],
            recv_sem=crecv.at[s, source],
            device_id=(k, g),
            device_id_type=MESH,
        )

    beside = (1, last - 1)

    def is_end(plane):
        return jnp.logical_or(plane == 0, plane == last)

    def inner(plane):
        return jnp.logical_and(plane > 0, plane < last)

    def m_copy(end, s, source):
        return pltpu.make_async_remote_copy(
            src_ref=c_send.at[end * last, s],
            dst_ref=c_mid.at[end, s, source],
            send_sem=csend.at[end * last, s],
            recv_sem=mrecv.at[end, s, source],
            device_id=(k, beside[end]),
            device_id_type=MESH,
        )

    side = lax.broadcasted_iota(jnp.int32, (packed_rows, shared), 1) // share_of

    def pack(block, core):
        top, bottom = block[:packed_rows], block[hours - packed_rows :]
        if core:
            top = pltpu.roll(top, share_of, 1)
        else:
            bottom = pltpu.roll(bottom, share_of, 1)
        return jnp.where(side == 0, top, bottom)

    def multiply(g, ch, slot):
        size = bounds[ch + 1] - bounds[ch]
        shared_in(g, ch).wait_recv()
        for half in range(PAIR):
            for b in range(held):
                z_work[half * held + b, 0:size, :] = z_all[
                    g, half, piece(ch), b * blk : (b + 1) * blk
                ]

        def product(i):
            total = None
            for s in range(each):
                term = lax.dot_general(
                    z_work[scalars[half_rows + i, s], 0:size, :],
                    f_all[i, s],
                    (((1,), (0,)), ((), ())),
                    preferred_element_type=jnp.float32,
                )
                total = term if total is None else total + term
            return total

        def one(e, carry):
            target = peer(e)
            s_send[slot, target, 0:size, :] = product(target).astype(s_send.dtype)
            s_copy(g, ch, slot, target, q).start()
            return carry

        lax.fori_loop(1, chips, one, 0)
        s_own[slot, 0:size, :] = product(q)

    def finish(p, ch):
        g = group_at(p)
        size = bounds[ch + 1] - bounds[ch]
        total = s_own[(p * CHUNKS + ch) % 2, 0:size, :]
        for e in range(1, chips):
            s_copy(g, ch, 0, q, peer(e)).wait_recv()
            total = total + s_all[g, ch, peer(e), 0:size, :].astype(jnp.float32)
        s_sum[bounds[ch] : bounds[ch + 1], :] = total
        for s in range(scens):
            if not bounds[ch] < (s + 1) * hours <= bounds[ch + 1]:
                continue
            spatial = s_sum[s * hours : (s + 1) * hours, :].astype(jnp.bfloat16)
            weather = jnp.dot(temporal_ref[...], spatial, preferred_element_type=jnp.float32)
            spread = spread_ref[...]
            values = scale_ref[...] * jnp.exp(spread * weather - 0.5 * spread * spread)
            sums = lax.dot_general(
                values.astype(jnp.bfloat16),
                onehot[...],
                (((1,), (1,)), ((), ())),
                preferred_element_type=jnp.float32,
            )

            @pl.when(p > 0)
            def _():
                for e in range(1, sites):
                    b_copy(g, s, seat(e), k).wait_send()

            for i in range(chips):
                block = sums[:, i * shared : (i + 1) * shared]
                for core in range(PAIR):
                    b_send[s, i * PAIR + core] = pack(block, core).astype(b_send.dtype)
            for e in range(1, sites):
                b_copy(g, s, seat(e), k).start()
            b_all[g, s, k] = b_send[s, k]

    def forward(p, s):
        g = group_at(p)
        for e in range(1, sites):
            b_copy(g, s, k, seat(e)).wait_recv()
        total = b_all[g, s, 0].astype(jnp.float32)
        for i in range(1, sites):
            total = total + b_all[g, s, i].astype(jnp.float32)

        @pl.when(p == 0)
        def _():
            c_all[s, z] = total

        @pl.when(p > 0)
        def _():
            c_send[g, s] = total

            @pl.when(jnp.logical_or(is_end(z), inner(g)))
            def _():
                c_copy(g, s, z).start()

            for end, near in enumerate(beside):

                @pl.when(jnp.logical_and(inner(z), jnp.logical_and(g == end * last, z != near)))
                def _():
                    m_copy(end, s, z).start()

    def free(g, ch, slot):
        for e in range(1, chips):
            s_copy(g, ch, slot, peer(e), q).wait_send()

    def done_in(s):
        return next(ch for ch in range(CHUNKS) if (s + 1) * hours <= bounds[ch + 1])

    def position(p, carry):
        g = group_at(p)
        for ch in range(CHUNKS):
            slot = (p * CHUNKS + ch) % 2
            if ch >= 2:
                free(g, ch - 2, slot)
            else:

                @pl.when(p > 0)
                def _():
                    free(g, ch + CHUNKS - 2, slot)

            multiply(g, ch, slot)
            for s in range(scens):
                at = done_in(s) + 3
                if at % CHUNKS == ch:

                    @pl.when(p >= at // CHUNKS)
                    def _():
                        forward(p - at // CHUNKS, s)

            if ch > 0:
                finish(p, ch - 1)
            else:

                @pl.when(p > 0)
                def _():
                    finish(p - 1, CHUNKS - 1)

            step = ch + 1
            if step < CHUNKS:

                @pl.when(p > 2)
                def _():
                    arrivals(p, step)
            else:

                @pl.when(jnp.logical_and(p >= 2, p < last))
                def _():
                    arrivals(p + 1, 0)

            if groups > 2 and ch in (CHUNKS - 2, CHUNKS - 1):
                early, part = (0, CHUNKS - 2) if ch == CHUNKS - 1 else (1, CHUNKS - 1)

                @pl.when(p == early)
                def _():
                    arrivals(2, part)

        return carry

    lax.fori_loop(0, groups, position, 0)
    for at in range(CHUNKS, CHUNKS + 3):
        if at == CHUNKS:
            finish(last, CHUNKS - 1)
        for s in range(scens):
            if done_in(s) + 3 == at:
                forward(last, s)

    for g in range(groups):
        for ch in range(CHUNKS):
            share(g, ch).wait_send()

            @pl.when(jnp.logical_and(g <= z, z < last))
            def _():
                hop(g, ch, 1).wait_send()

            @pl.when(jnp.logical_and(g >= z, z > 0))
            def _():
                hop(g, ch, 0).wait_send()

    for end, near in enumerate(beside):

        @pl.when(jnp.logical_and(inner(z), z == near))
        def _():
            for s in range(scens):
                total = c_send[end * last, s]
                for source in range(1, last):
                    if source != near:
                        m_copy(end, s, source).wait_recv()
                        total = total + c_mid[end, s, source]
                c_send[end * last, s] = total
                c_copy(end * last, s, z).start()

    def unpack(packed, s, ref):
        rest = pltpu.roll(packed[2 * packed_rows - hours :], share_of, 1)
        whole = jnp.concatenate([packed, rest], axis=0)
        ref[:, s * hours : (s + 1) * hours] = whole.T[:share_of]

    for s in range(scens):
        unpack(c_all[s, z], s, near_ref)
        c_sum[s] = jnp.zeros_like(c_sum[s])
    for d in range(1, groups):
        source = (z + d) % groups
        direct = jnp.logical_or(inner(z), is_end(source))
        for end, near in enumerate(beside):
            direct = jnp.logical_or(direct, jnp.logical_and(z == end * last, source == near))

        @pl.when(direct)
        def _():
            for s in range(scens):
                c_copy(z, s, source).wait_recv()
                c_sum[s] = c_sum[s] + c_all[s, source]

    for s in range(scens):
        unpack(c_sum[s], s, far_ref)

    free(z, CHUNKS - 2, (groups * CHUNKS - 2) % 2)
    free(z, CHUNKS - 1, (groups * CHUNKS - 1) % 2)
    for e in range(1, chips):
        f_copy(peer(e), q).wait_send()
    for s in range(scens):
        for e in range(1, sites):
            b_copy(z, s, seat(e), k).wait_send()
    for s in range(scens):
        for d in range(1, groups):
            c_copy((z + d) % groups, s, z).wait_send()


def bounds_of(width):
    small = width // 7
    large = (width - small) // (CHUNKS - 1)
    return [large * i for i in range(CHUNKS)] + [width]


def shards(normals, pattern, factor, temporal, capacity, spread, bus_map, buses):
    sites = lax.axis_size("site")
    groups = lax.axis_size("scen")
    depth, width = normals.shape
    rows_here, nz, height, blk = factor.shape
    hours = temporal.shape[0]
    scens = width // hours
    chips = sites // PAIR
    bounds = bounds_of(width)
    step = max(b - a for a, b in zip(bounds, bounds[1:]))
    slots = sites * MAX_COLUMN_BLOCKS
    each = slots // chips
    rows = rows_here * height
    shared = buses // chips
    packed_rows = (hours // 2 + 7) // 8 * 8
    block_count = depth // blk
    lanes = -(-block_count * sites // LANES) * LANES
    half_rows = -(-max(chips, rows_here) // 8) * 8

    bf16, f32, i32 = jnp.bfloat16, jnp.float32, jnp.int32
    dma = pltpu.SemaphoreType.DMA
    whole = pl.BlockSpec(memory_space=pltpu.VMEM)
    anywhere = pl.BlockSpec(memory_space=pl.ANY)
    near, far = pl.pallas_call(
        functools.partial(kernel, chips, groups, slots, hours),
        out_shape=[jax.ShapeDtypeStruct((buses // sites, width), f32)] * 2,
        in_specs=[anywhere] * 7,
        out_specs=[whole] * 2,
        scratch_shapes=[
            pltpu.VMEM(pattern.shape, i32),
            pltpu.VMEM(temporal.shape, bf16),
            pltpu.VMEM((capacity.size // LANES, LANES), f32),
            pltpu.VMEM((spread.size // LANES, LANES), f32),
            pltpu.VMEM((bus_map.size // LANES, LANES), i32),
            pltpu.VMEM((groups, PAIR, width, depth), bf16),
            pltpu.VMEM((PAIR * block_count, step, blk), bf16),
            pltpu.VMEM((rows_here, nz, height, blk), bf16),
            pltpu.VMEM((chips, each, blk, rows), bf16),
            pltpu.VMEM((chips, each, blk, rows), bf16),
            pltpu.VMEM((2, chips, step, rows), bf16),
            pltpu.VMEM((2, step, rows), f32),
            pltpu.VMEM((groups, CHUNKS, chips, step, rows), bf16),
            pltpu.VMEM((width, rows), f32),
            pltpu.VMEM((scens, sites, packed_rows, shared), bf16),
            pltpu.VMEM((groups, scens, sites, packed_rows, shared), bf16),
            pltpu.VMEM((groups, scens, packed_rows, shared), f32),
            pltpu.VMEM((scens, groups, packed_rows, shared), f32),
            pltpu.VMEM((2, scens, groups, packed_rows, shared), f32),
            pltpu.VMEM((scens, packed_rows, shared), f32),
            pltpu.VMEM((buses, rows), bf16),
            pltpu.VMEM((1, rows), f32),
            pltpu.VMEM((1, rows), f32),
            pltpu.VMEM((pattern.shape[0], lanes), i32),
            pltpu.VMEM((sites, lanes), i32),
            pltpu.VMEM((sites, lanes), i32),
            pltpu.VMEM((3, half_rows, lanes), i32),
            pltpu.VMEM((2 * half_rows, LANES), i32),
            pltpu.SMEM((2 * half_rows, LANES), i32),
            dma((8,)),
            dma((2, groups, CHUNKS)),
            dma((groups, CHUNKS)),
            dma((groups, CHUNKS)),
            dma((groups, CHUNKS)),
            dma((chips,)),
            dma((chips,)),
            dma((2, chips)),
            dma((groups, CHUNKS, chips)),
            dma((scens, sites)),
            dma((groups, scens, sites)),
            dma((groups, scens)),
            dma((scens, groups)),
            dma((2, scens, groups)),
            pltpu.SemaphoreType.REGULAR((max(chips.bit_length() - 2, 1),)),
        ],
        compiler_params=pltpu.CompilerParams(
            collective_id=0, has_side_effects=True, vmem_limit_bytes=VMEM_LIMIT
        ),
    )(
        pattern,
        normals.T,
        factor,
        temporal,
        capacity.reshape(-1, LANES),
        spread.reshape(-1, LANES),
        bus_map.reshape(-1, LANES),
    )
    return near + far


def solution(mesh):
    placed = (P("site", "scen"), P(), P("site", None, "scen", None), P(), P("site"), P("site"), P())
    sites = mesh.shape["site"]

    def whole(normals, pattern, factor, temporal, capacity, spread, bus_map):
        buses = factor.shape[0] * factor.shape[3] // 16

        def body(*args):
            return shards(*args, buses)

        return jax.shard_map(
            body, mesh=mesh, in_specs=placed, out_specs=P("site", "scen"), check_vma=False
        )(normals, pattern, factor, temporal, capacity, spread, bus_map)

    return whole
```

```python
import functools
import math

import jax
import jax.numpy as jnp
from jax import lax
from jax.experimental import pallas as pl
from jax.experimental.pallas import tpu as pltpu
from jax.sharding import PartitionSpec as P

MAX_COLUMN_BLOCKS = 5
PAIR = 2
CHUNKS = 3
LANES = 128
VMEM_LIMIT = 67043328
VMEM_MARGIN = 3 * 1024 * 1024
MESH = pl.DeviceIdType.MESH


def kernel(
    chips,
    groups,
    slots,
    hours,
    pattern_hbm,
    z_ref,
    f_ref,
    temporal_hbm,
    capacity_hbm,
    spreads_hbm,
    buses_hbm,
    near_ref,
    far_ref,
    pattern_ref,
    temporal_ref,
    capacity_ref,
    spreads_ref,
    buses_ref,
    z_all,
    z_work,
    f_raw,
    f_sorted,
    f_all,
    s_send,
    s_own,
    s_all,
    s_sum,
    b_send,
    b_all,
    c_send,
    c_all,
    c_mid,
    c_sum,
    onehot,
    scale_ref,
    spread_ref,
    pos,
    need,
    ranks,
    gathered,
    tables,
    scalars,
    local_sem,
    zsend,
    zrecv,
    psend,
    precv,
    fsend,
    frecv,
    ssend,
    srecv,
    bsend,
    brecv,
    csend,
    crecv,
    mrecv,
    meet,
):
    k = lax.axis_index("site")
    z = lax.axis_index("scen")
    q = k // PAIR
    c = k % PAIR
    other = q * PAIR + (PAIR - 1 - c)
    rows_here, nz, height, blk = f_ref.shape
    width, depth = z_ref.shape
    bounds = bounds_of(width)
    each = slots // chips
    scens = width // hours
    share_of = near_ref.shape[0]
    shared = share_of * PAIR
    packed_rows = b_send.shape[2]
    sites = chips * PAIR
    held = depth // blk
    lanes = pos.shape[1]
    rows = rows_here * height
    last = groups - 1

    bits = [1 << i for i in range(chips.bit_length() - 1)]

    def across(bit):
        return q + bit - 2 * bit * ((q // bit) % 2)

    barrier = pltpu.get_barrier_semaphore()

    def peer(e):
        return (q + e) % chips

    def greet(device):
        pl.semaphore_signal(barrier, inc=1, device_id=device, device_id_type=MESH)

    @pl.when(z < last)
    def _():
        greet((k, z + 1))

    @pl.when(z > 0)
    def _():
        greet((k, z - 1))

    greet((other, z))
    for bit in bits:
        greet((across(bit) * PAIR + c, z))

    small = [
        (pattern_hbm, pattern_ref),
        (temporal_hbm, temporal_ref),
        (capacity_hbm, capacity_ref),
        (spreads_hbm, spreads_ref),
        (buses_hbm, buses_ref),
    ]
    loads = [
        pltpu.make_async_copy(source, target, local_sem.at[3 + i])
        for i, (source, target) in enumerate(small)
    ]
    for load in loads:
        load.start()
    ends = jnp.where(z < last, 1, 0) + jnp.where(z > 0, 1, 0)
    pl.semaphore_wait(barrier, 1 + len(bits) + ends)

    def piece(ch):
        return pl.ds(bounds[ch], bounds[ch + 1] - bounds[ch])

    def hop(g, ch, up, source=None):
        part = z_all.at[g, c, piece(ch)]
        return pltpu.make_async_remote_copy(
            src_ref=part if source is None else source,
            dst_ref=part,
            send_sem=zsend.at[up, g, ch],
            recv_sem=zrecv.at[g, ch],
            device_id=(k, z + 1 if up else z - 1),
            device_id_type=MESH,
        )

    def share(g, ch, source=None):
        part = z_all.at[g, c, piece(ch)]
        return pltpu.make_async_remote_copy(
            src_ref=part if source is None else source,
            dst_ref=part,
            send_sem=psend.at[g, ch],
            recv_sem=precv.at[g, ch],
            device_id=(other, z),
            device_id_type=MESH,
        )

    def came_in(g, ch):
        part = z_all.at[g, c, piece(ch)]
        return pltpu.make_async_remote_copy(
            src_ref=part,
            dst_ref=part,
            send_sem=psend.at[g, ch],
            recv_sem=zrecv.at[g, ch],
            device_id=(other, z),
            device_id_type=MESH,
        )

    def shared_in(g, ch):
        part = z_all.at[g, 1 - c, piece(ch)]
        return pltpu.make_async_remote_copy(
            src_ref=part,
            dst_ref=part,
            send_sem=psend.at[g, ch],
            recv_sem=precv.at[g, ch],
            device_id=(other, z),
            device_id_type=MESH,
        )

    for ch in range(CHUNKS):
        own = z_ref.at[piece(ch)]
        late = ch == CHUNKS - 1

        @pl.when(z < (last - 1 if late else last))
        def _():
            hop(z, ch, 1, own).start()

        @pl.when(z > (1 if late else 0))
        def _():
            hop(z, ch, 0, own).start()

    for ch in range(CHUNKS):
        share(z, ch, z_ref.at[piece(ch)]).start()

    for i, bit in enumerate(bits[:-1]):
        pl.semaphore_signal(
            meet.at[i], inc=1, device_id=(across(bit) * PAIR + c, z), device_id_type=MESH
        )
        pl.semaphore_wait(meet.at[i], 1)

    z_load = pltpu.make_async_copy(z_ref, z_all.at[z, c], local_sem.at[0])
    z_load.start()
    f_load = pltpu.make_async_copy(f_ref, f_raw, local_sem.at[1])
    f_load.start()
    for load in loads:
        load.wait()

    lane = lax.broadcasted_iota(jnp.int32, (1, lanes), 1)
    owner = jnp.zeros_like(lane)
    for j in range(1, sites):
        owner = owner + jnp.where(lane >= j * held, 1, 0)
    local = lane - owner * held
    found = jnp.zeros(pos.shape, jnp.int32)
    for t in range(nz):
        found = jnp.where(pattern_ref[:, t : t + 1] == lane, t + 1, found)
    pos[...] = found
    for i in range(sites):
        line = pos[i * rows_here : i * rows_here + 1, :]
        for r in range(1, rows_here):
            at = i * rows_here + r
            line = jnp.maximum(line, pos[at : at + 1, :])
        need[i : i + 1, :] = jnp.where(line > 0, 1, 0)
    wanted = need[...]
    before = jnp.zeros_like(wanted)
    for d in range(1, held):
        before = before + jnp.where(local >= d, pltpu.roll(wanted, d, 1), 0)
    ranks[...] = before

    half_rows = tables.shape[0] // 2
    column = lax.broadcasted_iota(jnp.int32, (half_rows, tables.shape[1]), 1)
    gathered[...] = jnp.zeros_like(gathered)
    for r in range(rows_here):
        gathered[0, r : r + 1, :] = pos[pl.ds(k * rows_here + r, 1), :]
    for i in range(chips):
        gathered[1, i : i + 1, :] = need[pl.ds(i * PAIR + c, 1), :]
        gathered[2, i : i + 1, :] = ranks[pl.ds(i * PAIR + c, 1), :]
    own_slot = owner * MAX_COLUMN_BLOCKS + ranks[pl.ds(k, 1), :]
    own_slot = jnp.where(need[pl.ds(k, 1), :] > 0, own_slot, -1)
    places = jnp.zeros(column.shape, jnp.int32)
    positions = gathered[0]
    for t in range(slots):
        at = jnp.sum(jnp.where(own_slot == t, positions, 0), axis=1, keepdims=True)
        places = jnp.where(column == t, at, places)
    tables[0:half_rows, :] = places - 1
    blocks = jnp.zeros(column.shape, jnp.int32)
    needs, orders = gathered[1], gathered[2]
    first = q * PAIR * held
    for half in range(PAIR):
        mine = jnp.where(owner == q * PAIR + half, needs, 0)
        for j in range(MAX_COLUMN_BLOCKS):
            hit = jnp.where(orders == j, mine, 0)
            at = jnp.sum(hit * (lane - first), axis=1, keepdims=True)
            blocks = jnp.where(column == half * MAX_COLUMN_BLOCKS + j, at, blocks)
    tables[half_rows:, :] = blocks
    t_load = pltpu.make_async_copy(tables, scalars, local_sem.at[2])
    t_load.start()

    narrow = capacity_ref.shape[1]
    narrow_lane = lax.broadcasted_iota(jnp.int32, (8, narrow), 1)
    offset = z * height

    def rows_of(ref, base):
        parts = []
        for start in range(0, rows, narrow):
            part = None
            for r in range(start // height, min((start + narrow) // height, rows_here)):
                line = ref[pl.ds(base + r * blk // narrow + offset // narrow, 1), :]
                line = jnp.broadcast_to(line, narrow_lane.shape)
                shift = (r * height - start + narrow - offset % narrow) % narrow
                line = pltpu.roll(line, shift, 1)
                if part is None:
                    part = line
                else:
                    part = jnp.where(narrow_lane >= r * height - start, line, part)
            parts.append(part[0:1])
        return jnp.concatenate(parts, axis=1) if len(parts) > 1 else parts[0]

    scale_ref[...] = rows_of(capacity_ref, 0)
    spread_ref[...] = rows_of(spreads_ref, 0)
    maps = rows_of(buses_ref, k * (rows_here * blk // narrow))
    bus_ids = lax.broadcasted_iota(jnp.int32, onehot.shape, 0)
    onehot[...] = jnp.where(bus_ids == maps, 1.0, 0.0).astype(onehot.dtype)
    t_load.wait()

    def relay(g, ch):
        came_in(g, ch).wait_recv()

        @pl.when(jnp.logical_and(g < z, z < last))
        def _():
            hop(g, ch, 1).start()

        @pl.when(jnp.logical_and(g > z, z > 0))
        def _():
            hop(g, ch, 0).start()

        share(g, ch).start()

    def arrivals(d, ch):
        @pl.when(z - d >= 0)
        def _():
            relay(z - d, ch)

        @pl.when(z + d <= last)
        def _():
            relay(z + d, ch)

        if ch == CHUNKS - 1:
            own = z_ref.at[piece(ch)]

            @pl.when(jnp.logical_and(d == last - 1, z == 1))
            def _():
                hop(z, ch, 0, own).start()

            @pl.when(jnp.logical_and(d == last - 1, z == last - 1))
            def _():
                hop(z, ch, 1, own).start()

    def f_copy(target, source):
        return pltpu.make_async_remote_copy(
            src_ref=f_sorted.at[target],
            dst_ref=f_all.at[source],
            send_sem=fsend.at[target],
            recv_sem=frecv.at[source],
            device_id=(target * PAIR + c, z),
            device_id_type=MESH,
        )

    f_load.wait()

    def sort_for(target, store):
        def one(s, carry):
            blocks = []
            for r in range(rows_here):
                t = scalars[r, target * each + s]
                block = f_raw[r, jnp.maximum(t, 0)]
                if slots > nz:
                    block = jnp.where(t >= 0, block, jnp.zeros_like(block))
                blocks.append(block)
            store(s, jnp.concatenate(blocks, axis=0).T)
            return carry

        lax.fori_loop(0, each, one, 0)

    for e in range(1, chips):
        target = peer(e)

        def to_send(s, tile):
            f_sorted[target, s] = tile

        sort_for(target, to_send)
        f_copy(target, q).start()

    def to_own(s, tile):
        f_all[q, s] = tile

    sort_for(q, to_own)

    z_load.wait()

    for ch in range(CHUNKS - 1):
        arrivals(1, ch)

    @pl.when(jnp.logical_and(z > 0, z < last))
    def _():
        arrivals(1, CHUNKS - 1)

    arrivals(2, 0)
    for e in range(1, chips):
        f_copy(q, peer(e)).wait_recv()

    fewer = jnp.minimum(z, last - z)
    more = jnp.where(z < last - z, 1, -1)

    def group_at(p):
        near = jnp.where(p % 2 == 1, -((p + 1) // 2), (p + 1) // 2)
        far = more * (p - fewer)
        return z + jnp.where(p <= 2 * fewer, near, far)

    def s_copy(g, ch, slot, target, source):
        size = bounds[ch + 1] - bounds[ch]
        return pltpu.make_async_remote_copy(
            src_ref=s_send.at[slot, target, pl.ds(0, size)],
            dst_ref=s_all.at[g, ch, source, pl.ds(0, size)],
            send_sem=ssend.at[slot, target],
            recv_sem=srecv.at[g, ch, source],
            device_id=(target * PAIR + c, z),
            device_id_type=MESH,
        )

    def b_copy(g, s, target, source):
        return pltpu.make_async_remote_copy(
            src_ref=b_send.at[s, target],
            dst_ref=b_all.at[g, s, source],
            send_sem=bsend.at[s, target],
            recv_sem=brecv.at[g, s, source],
            device_id=(target, z),
            device_id_type=MESH,
        )

    def seat(e):
        return (k + e) % sites

    def c_copy(g, s, source):
        return pltpu.make_async_remote_copy(
            src_ref=c_send.at[g, s],
            dst_ref=c_all.at[s, source],
            send_sem=csend.at[g, s],
            recv_sem=crecv.at[s, source],
            device_id=(k, g),
            device_id_type=MESH,
        )

    beside = (1, last - 1)

    def is_end(plane):
        return jnp.logical_or(plane == 0, plane == last)

    def inner(plane):
        return jnp.logical_and(plane > 0, plane < last)

    def m_copy(end, s, source):
        return pltpu.make_async_remote_copy(
            src_ref=c_send.at[end * last, s],
            dst_ref=c_mid.at[end, s, source],
            send_sem=csend.at[end * last, s],
            recv_sem=mrecv.at[end, s, source],
            device_id=(k, beside[end]),
            device_id_type=MESH,
        )

    side = lax.broadcasted_iota(jnp.int32, (packed_rows, shared), 1) // share_of

    def pack(block, core):
        top, bottom = block[:packed_rows], block[hours - packed_rows :]
        if core:
            top = pltpu.roll(top, share_of, 1)
        else:
            bottom = pltpu.roll(bottom, share_of, 1)
        return jnp.where(side == 0, top, bottom)

    def multiply(g, ch, slot):
        size = bounds[ch + 1] - bounds[ch]
        shared_in(g, ch).wait_recv()
        for half in range(PAIR):
            for b in range(held):
                z_work[half * held + b, 0:size, :] = z_all[
                    g, half, piece(ch), b * blk : (b + 1) * blk
                ]

        def product(i):
            total = None
            for s in range(each):
                term = lax.dot_general(
                    z_work[scalars[half_rows + i, s], 0:size, :],
                    f_all[i, s],
                    (((1,), (0,)), ((), ())),
                    preferred_element_type=jnp.float32,
                )
                total = term if total is None else total + term
            return total

        def one(e, carry):
            target = peer(e)
            s_send[slot, target, 0:size, :] = product(target).astype(s_send.dtype)
            s_copy(g, ch, slot, target, q).start()
            return carry

        lax.fori_loop(1, chips, one, 0)
        s_own[slot, 0:size, :] = product(q)

    def lane_of(p):
        return jnp.where(p == 1, 1, 0)

    def finish(p, ch):
        g = group_at(p)
        size = bounds[ch + 1] - bounds[ch]
        total = s_own[ch, 0:size, :]
        for e in range(1, chips):
            s_copy(g, ch, 0, q, peer(e)).wait_recv()
            total = total + s_all[g, ch, peer(e), 0:size, :].astype(jnp.float32)
        s_sum[lane_of(p), bounds[ch] : bounds[ch + 1], :] = total
        for s in range(scens):
            if not bounds[ch] < (s + 1) * hours <= bounds[ch + 1]:
                continue
            spatial = s_sum[lane_of(p), s * hours : (s + 1) * hours, :].astype(jnp.bfloat16)
            weather = jnp.dot(temporal_ref[...], spatial, preferred_element_type=jnp.float32)
            spread = spread_ref[...]
            values = scale_ref[...] * jnp.exp(spread * weather - 0.5 * spread * spread)
            sums = lax.dot_general(
                values.astype(jnp.bfloat16),
                onehot[...],
                (((1,), (1,)), ((), ())),
                preferred_element_type=jnp.float32,
            )

            @pl.when(p > 0)
            def _():
                for e in range(1, sites):
                    b_copy(g, s, seat(e), k).wait_send()

            for i in range(chips):
                block = sums[:, i * shared : (i + 1) * shared]
                for core in range(PAIR):
                    b_send[s, i * PAIR + core] = pack(block, core).astype(b_send.dtype)
            for e in range(1, sites):
                b_copy(g, s, seat(e), k).start()
            b_all[g, s, k] = b_send[s, k]

    def forward(p, s):
        g = group_at(p)
        for e in range(1, sites):
            b_copy(g, s, k, seat(e)).wait_recv()
        total = b_all[g, s, 0].astype(jnp.float32)
        for i in range(1, sites):
            total = total + b_all[g, s, i].astype(jnp.float32)

        @pl.when(p == 0)
        def _():
            c_all[s, z] = total

        @pl.when(p > 0)
        def _():
            c_send[g, s] = total

            @pl.when(jnp.logical_or(is_end(z), inner(g)))
            def _():
                c_copy(g, s, z).start()

            for end, near in enumerate(beside):

                @pl.when(jnp.logical_and(inner(z), jnp.logical_and(g == end * last, z != near)))
                def _():
                    m_copy(end, s, z).start()

    def free(g, ch, slot):
        for e in range(1, chips):
            s_copy(g, ch, slot, peer(e), q).wait_send()

    def done_in(s):
        return next(ch for ch in range(CHUNKS) if (s + 1) * hours <= bounds[ch + 1])

    final = CHUNKS - 1

    def stage(p, ch):
        g = group_at(p)

        @pl.when(p > 0)
        def _():
            free(g, ch, ch)

        multiply(g, ch, ch)

    def position(p, carry):
        for ch in range(CHUNKS):
            if ch == final:

                @pl.when(p != 1)
                def _():
                    stage(p, ch)

            else:
                stage(p, ch)
            for s in range(scens):
                at = done_in(s) + 3
                if at % CHUNKS == ch:
                    back = at // CHUNKS
                    ready = p >= back
                    if done_in(s) == final:
                        ready = jnp.logical_and(ready, p != 1 + back)

                    @pl.when(ready)
                    def _():
                        forward(p - back, s)

            if ch > 0:
                finish(p, ch - 1)
            else:

                @pl.when(jnp.logical_and(p > 0, p != 2))
                def _():
                    finish(p - 1, final)

            step = ch + 1
            if step < CHUNKS:

                @pl.when(p > 2)
                def _():
                    arrivals(p, step)
            else:

                @pl.when(jnp.logical_and(p >= 2, p < last))
                def _():
                    arrivals(p + 1, 0)

            for part in range(1, CHUNKS):
                if 2 * part % CHUNKS == ch:

                    @pl.when(p == 2 * part // CHUNKS)
                    def _():
                        arrivals(2, part)

        return carry

    lax.fori_loop(0, groups, position, 0)
    finish(last, final)

    @pl.when(is_end(z))
    def _():
        arrivals(1, final)

    for s in range(scens):
        if done_in(s) < final and done_in(s) + 3 >= CHUNKS:
            forward(last, s)
    stage(1, final)
    for s in range(scens):
        if done_in(s) == final:
            forward(last, s)
    finish(1, final)
    for s in range(scens):
        if done_in(s) == final:
            forward(1, s)

    for g in range(groups):
        for ch in range(CHUNKS):
            share(g, ch).wait_send()

            @pl.when(jnp.logical_and(g <= z, z < last))
            def _():
                hop(g, ch, 1).wait_send()

            @pl.when(jnp.logical_and(g >= z, z > 0))
            def _():
                hop(g, ch, 0).wait_send()

    for end, near in enumerate(beside):

        @pl.when(jnp.logical_and(inner(z), z == near))
        def _():
            for s in range(scens):
                total = c_send[end * last, s]
                for source in range(1, last):
                    if source != near:
                        m_copy(end, s, source).wait_recv()
                        total = total + c_mid[end, s, source]
                c_send[end * last, s] = total
                c_copy(end * last, s, z).start()

    def unpack(packed, s, ref):
        rest = pltpu.roll(packed[2 * packed_rows - hours :], share_of, 1)
        whole = jnp.concatenate([packed, rest], axis=0)
        ref[:, s * hours : (s + 1) * hours] = whole.T[:share_of]

    for s in range(scens):
        unpack(c_all[s, z], s, near_ref)
        c_sum[s] = jnp.zeros_like(c_sum[s])
    for s in range(scens):
        for d in range(1, groups):
            source = (z + d) % groups
            direct = jnp.logical_or(inner(z), is_end(source))
            for end, near in enumerate(beside):
                direct = jnp.logical_or(direct, jnp.logical_and(z == end * last, source == near))

            @pl.when(direct)
            def _():
                c_copy(z, s, source).wait_recv()
                c_sum[s] = c_sum[s] + c_all[s, source]

        unpack(c_sum[s], s, far_ref)

    for ch in range(CHUNKS):
        free(z, ch, ch)
    for e in range(1, chips):
        f_copy(peer(e), q).wait_send()
    for s in range(scens):
        for e in range(1, sites):
            b_copy(z, s, seat(e), k).wait_send()
    for s in range(scens):
        for d in range(1, groups):
            c_copy((z + d) % groups, s, z).wait_send()


def bounds_of(width):
    unit = width // 21
    return [0, 8 * unit, 17 * unit, width]


def shards(normals, pattern, factor, temporal, capacity, spread, bus_map, buses):
    sites = lax.axis_size("site")
    groups = lax.axis_size("scen")
    depth, width = normals.shape
    rows_here, nz, height, blk = factor.shape
    hours = temporal.shape[0]
    scens = width // hours
    chips = sites // PAIR
    bounds = bounds_of(width)
    step = max(b - a for a, b in zip(bounds, bounds[1:]))
    slots = sites * MAX_COLUMN_BLOCKS
    each = slots // chips
    rows = rows_here * height
    shared = buses // chips
    packed_rows = (hours // 2 + 7) // 8 * 8
    block_count = depth // blk
    lanes = -(-block_count * sites // LANES) * LANES
    half_rows = -(-max(chips, rows_here) // 8) * 8

    bf16, f32, i32 = jnp.bfloat16, jnp.float32, jnp.int32
    dma = pltpu.SemaphoreType.DMA
    whole = pl.BlockSpec(memory_space=pltpu.VMEM)
    anywhere = pl.BlockSpec(memory_space=pltpu.HBM)
    scratch = [
        pltpu.VMEM(pattern.shape, i32),
        pltpu.VMEM(temporal.shape, bf16),
        pltpu.VMEM((capacity.size // LANES, LANES), f32),
        pltpu.VMEM((spread.size // LANES, LANES), f32),
        pltpu.VMEM((bus_map.size // LANES, LANES), i32),
        pltpu.VMEM((groups, PAIR, width, depth), bf16),
        pltpu.VMEM((PAIR * block_count, step, blk), bf16),
        pltpu.VMEM((rows_here, nz, height, blk), bf16),
        pltpu.VMEM((chips, each, blk, rows), bf16),
        pltpu.VMEM((chips, each, blk, rows), bf16),
        pltpu.VMEM((CHUNKS, chips, step, rows), bf16),
        pltpu.VMEM((CHUNKS, step, rows), f32),
        pltpu.VMEM((groups, CHUNKS, chips, step, rows), bf16),
        pltpu.VMEM((2, width, rows), f32),
        pltpu.VMEM((scens, sites, packed_rows, shared), bf16),
        pltpu.VMEM((groups, scens, sites, packed_rows, shared), bf16),
        pltpu.VMEM((groups, scens, packed_rows, shared), f32),
        pltpu.VMEM((scens, groups, packed_rows, shared), f32),
        pltpu.VMEM((2, scens, groups, packed_rows, shared), f32),
        pltpu.VMEM((scens, packed_rows, shared), f32),
        pltpu.VMEM((buses, rows), bf16),
        pltpu.VMEM((1, rows), f32),
        pltpu.VMEM((1, rows), f32),
        pltpu.VMEM((pattern.shape[0], lanes), i32),
        pltpu.VMEM((sites, lanes), i32),
        pltpu.VMEM((sites, lanes), i32),
        pltpu.VMEM((3, half_rows, lanes), i32),
        pltpu.VMEM((2 * half_rows, LANES), i32),
        pltpu.SMEM((2 * half_rows, LANES), i32),
        dma((8,)),
        dma((2, groups, CHUNKS)),
        dma((groups, CHUNKS)),
        dma((groups, CHUNKS)),
        dma((groups, CHUNKS)),
        dma((chips,)),
        dma((chips,)),
        dma((CHUNKS, chips)),
        dma((groups, CHUNKS, chips)),
        dma((scens, sites)),
        dma((groups, scens, sites)),
        dma((groups, scens)),
        dma((scens, groups)),
        dma((2, scens, groups)),
        pltpu.SemaphoreType.REGULAR((max(chips.bit_length() - 2, 1),)),
    ]
    taken = sum(
        math.prod(ref.shape) * ref.dtype.itemsize
        for ref in scratch
        if ref.memory_space == pltpu.VMEM
    )
    limit = min(taken + taken // 16 + VMEM_MARGIN, VMEM_LIMIT)
    near, far = pl.pallas_call(
        functools.partial(kernel, chips, groups, slots, hours),
        out_shape=[jax.ShapeDtypeStruct((buses // sites, width), f32)] * 2,
        in_specs=[anywhere] * 7,
        out_specs=[whole] * 2,
        scratch_shapes=scratch,
        compiler_params=pltpu.CompilerParams(
            collective_id=0, has_side_effects=True, vmem_limit_bytes=limit
        ),
    )(
        *(
            pltpu.with_memory_space_constraint(x, pltpu.HBM)
            for x in (
                pattern,
                normals.T,
                factor,
                temporal,
                capacity.reshape(-1, LANES),
                spread.reshape(-1, LANES),
                bus_map.reshape(-1, LANES),
            )
        )
    )
    return near + far


def solution(mesh):
    placed = (P("site", "scen"), P(), P("site", None, "scen", None), P(), P("site"), P("site"), P())
    sites = mesh.shape["site"]

    def whole(normals, pattern, factor, temporal, capacity, spread, bus_map):
        buses = factor.shape[0] * factor.shape[3] // 16

        def body(*args):
            return shards(*args, buses)

        return jax.shard_map(
            body, mesh=mesh, in_specs=placed, out_specs=P("site", "scen"), check_vma=False
        )(normals, pattern, factor, temporal, capacity, spread, bus_map)

    return whole
```

```python
import functools
import math

import jax
import jax.numpy as jnp
from jax import lax
from jax.experimental import pallas as pl
from jax.experimental.pallas import tpu as pltpu
from jax.sharding import PartitionSpec as P

MAX_COLUMN_BLOCKS = 5
PAIR = 2
CHUNKS = 3
LANES = 128
VMEM_LIMIT = 67043328
VMEM_MARGIN = 3 * 1024 * 1024
MESH = pl.DeviceIdType.MESH


def kernel(
    chips,
    groups,
    slots,
    hours,
    pattern_hbm,
    z_ref,
    f_ref,
    temporal_hbm,
    capacity_hbm,
    spreads_hbm,
    buses_hbm,
    near_ref,
    far_ref,
    pattern_ref,
    temporal_ref,
    capacity_ref,
    spreads_ref,
    buses_ref,
    z_all,
    z_work,
    f_raw,
    f_sorted,
    f_all,
    s_send,
    s_own,
    s_all,
    s_sum,
    b_send,
    b_all,
    c_send,
    c_all,
    c_mid,
    c_sum,
    onehot,
    scale_ref,
    spread_ref,
    pos,
    need,
    ranks,
    gathered,
    tables,
    scalars,
    local_sem,
    zsend,
    zrecv,
    psend,
    precv,
    fsend,
    frecv,
    ssend,
    srecv,
    bsend,
    brecv,
    csend,
    crecv,
    mrecv,
    meet,
):
    k = lax.axis_index("site")
    z = lax.axis_index("scen")
    q = k // PAIR
    c = k % PAIR
    other = q * PAIR + (PAIR - 1 - c)
    rows_here, nz, height, blk = f_ref.shape
    width, depth = z_ref.shape
    bounds = bounds_of(width)
    each = slots // chips
    scens = width // hours
    share_of = near_ref.shape[0]
    shared = share_of * PAIR
    packed_rows = b_send.shape[2]
    sites = chips * PAIR
    held = depth // blk
    lanes = pos.shape[1]
    rows = rows_here * height
    last = groups - 1

    bits = [1 << i for i in range(chips.bit_length() - 1)]

    def across(bit):
        return q + bit - 2 * bit * ((q // bit) % 2)

    barrier = pltpu.get_barrier_semaphore()

    def peer(e):
        return (q + e) % chips

    def greet(device):
        pl.semaphore_signal(barrier, inc=1, device_id=device, device_id_type=MESH)

    @pl.when(z < last)
    def _():
        greet((k, z + 1))

    @pl.when(z > 0)
    def _():
        greet((k, z - 1))

    greet((other, z))
    for bit in bits:
        greet((across(bit) * PAIR + c, z))

    small = [
        (pattern_hbm, pattern_ref),
        (temporal_hbm, temporal_ref),
        (capacity_hbm, capacity_ref),
        (spreads_hbm, spreads_ref),
        (buses_hbm, buses_ref),
    ]
    loads = [
        pltpu.make_async_copy(source, target, local_sem.at[3 + i])
        for i, (source, target) in enumerate(small)
    ]
    for load in loads:
        load.start()
    ends = jnp.where(z < last, 1, 0) + jnp.where(z > 0, 1, 0)
    pl.semaphore_wait(barrier, 1 + len(bits) + ends)

    def piece(ch):
        return pl.ds(bounds[ch], bounds[ch + 1] - bounds[ch])

    def hop(g, ch, up, source=None):
        part = z_all.at[g, c, piece(ch)]
        return pltpu.make_async_remote_copy(
            src_ref=part if source is None else source,
            dst_ref=part,
            send_sem=zsend.at[up, g, ch],
            recv_sem=zrecv.at[g, ch],
            device_id=(k, z + 1 if up else z - 1),
            device_id_type=MESH,
        )

    def share(g, ch, source=None):
        part = z_all.at[g, c, piece(ch)]
        return pltpu.make_async_remote_copy(
            src_ref=part if source is None else source,
            dst_ref=part,
            send_sem=psend.at[g, ch],
            recv_sem=precv.at[g, ch],
            device_id=(other, z),
            device_id_type=MESH,
        )

    def came_in(g, ch):
        part = z_all.at[g, c, piece(ch)]
        return pltpu.make_async_remote_copy(
            src_ref=part,
            dst_ref=part,
            send_sem=psend.at[g, ch],
            recv_sem=zrecv.at[g, ch],
            device_id=(other, z),
            device_id_type=MESH,
        )

    def shared_in(g, ch):
        part = z_all.at[g, 1 - c, piece(ch)]
        return pltpu.make_async_remote_copy(
            src_ref=part,
            dst_ref=part,
            send_sem=psend.at[g, ch],
            recv_sem=precv.at[g, ch],
            device_id=(other, z),
            device_id_type=MESH,
        )

    for ch in range(CHUNKS):
        own = z_ref.at[piece(ch)]
        late = ch == CHUNKS - 1

        @pl.when(z < (last - 1 if late else last))
        def _():
            hop(z, ch, 1, own).start()

        @pl.when(z > (1 if late else 0))
        def _():
            hop(z, ch, 0, own).start()

    for ch in range(CHUNKS):
        share(z, ch, z_ref.at[piece(ch)]).start()

    for i, bit in enumerate(bits[:-1]):
        pl.semaphore_signal(
            meet.at[i], inc=1, device_id=(across(bit) * PAIR + c, z), device_id_type=MESH
        )
        pl.semaphore_wait(meet.at[i], 1)

    z_load = pltpu.make_async_copy(z_ref, z_all.at[z, c], local_sem.at[0])
    z_load.start()
    f_load = pltpu.make_async_copy(f_ref, f_raw, local_sem.at[1])
    f_load.start()
    for load in loads:
        load.wait()

    lane = lax.broadcasted_iota(jnp.int32, (1, lanes), 1)
    owner = jnp.zeros_like(lane)
    for j in range(1, sites):
        owner = owner + jnp.where(lane >= j * held, 1, 0)
    local = lane - owner * held
    found = jnp.zeros(pos.shape, jnp.int32)
    for t in range(nz):
        found = jnp.where(pattern_ref[:, t : t + 1] == lane, t + 1, found)
    pos[...] = found
    for i in range(sites):
        line = pos[i * rows_here : i * rows_here + 1, :]
        for r in range(1, rows_here):
            at = i * rows_here + r
            line = jnp.maximum(line, pos[at : at + 1, :])
        need[i : i + 1, :] = jnp.where(line > 0, 1, 0)
    wanted = need[...]
    before = jnp.zeros_like(wanted)
    for d in range(1, held):
        before = before + jnp.where(local >= d, pltpu.roll(wanted, d, 1), 0)
    ranks[...] = before

    half_rows = tables.shape[0] // 2
    column = lax.broadcasted_iota(jnp.int32, (half_rows, tables.shape[1]), 1)
    gathered[...] = jnp.zeros_like(gathered)
    for r in range(rows_here):
        gathered[0, r : r + 1, :] = pos[pl.ds(k * rows_here + r, 1), :]
    for i in range(chips):
        gathered[1, i : i + 1, :] = need[pl.ds(i * PAIR + c, 1), :]
        gathered[2, i : i + 1, :] = ranks[pl.ds(i * PAIR + c, 1), :]
    own_slot = owner * MAX_COLUMN_BLOCKS + ranks[pl.ds(k, 1), :]
    own_slot = jnp.where(need[pl.ds(k, 1), :] > 0, own_slot, -1)
    places = jnp.zeros(column.shape, jnp.int32)
    positions = gathered[0]
    for t in range(slots):
        at = jnp.sum(jnp.where(own_slot == t, positions, 0), axis=1, keepdims=True)
        places = jnp.where(column == t, at, places)
    tables[0:half_rows, :] = places - 1
    blocks = jnp.zeros(column.shape, jnp.int32)
    needs, orders = gathered[1], gathered[2]
    first = q * PAIR * held
    for half in range(PAIR):
        mine = jnp.where(owner == q * PAIR + half, needs, 0)
        for j in range(MAX_COLUMN_BLOCKS):
            hit = jnp.where(orders == j, mine, 0)
            at = jnp.sum(hit * (lane - first), axis=1, keepdims=True)
            blocks = jnp.where(column == half * MAX_COLUMN_BLOCKS + j, at, blocks)
    tables[half_rows:, :] = blocks
    t_load = pltpu.make_async_copy(tables, scalars, local_sem.at[2])
    t_load.start()

    narrow = capacity_ref.shape[1]
    narrow_lane = lax.broadcasted_iota(jnp.int32, (8, narrow), 1)
    offset = z * height

    def rows_of(ref, base):
        parts = []
        for start in range(0, rows, narrow):
            part = None
            for r in range(start // height, min((start + narrow) // height, rows_here)):
                line = ref[pl.ds(base + r * blk // narrow + offset // narrow, 1), :]
                line = jnp.broadcast_to(line, narrow_lane.shape)
                shift = (r * height - start + narrow - offset % narrow) % narrow
                line = pltpu.roll(line, shift, 1)
                if part is None:
                    part = line
                else:
                    part = jnp.where(narrow_lane >= r * height - start, line, part)
            parts.append(part[0:1])
        return jnp.concatenate(parts, axis=1) if len(parts) > 1 else parts[0]

    scale_ref[...] = rows_of(capacity_ref, 0)
    spread_ref[...] = rows_of(spreads_ref, 0)
    maps = rows_of(buses_ref, k * (rows_here * blk // narrow))
    bus_ids = lax.broadcasted_iota(jnp.int32, onehot.shape, 0)
    onehot[...] = jnp.where(bus_ids == maps, 1.0, 0.0).astype(onehot.dtype)
    t_load.wait()

    def relay(g, ch):
        came_in(g, ch).wait_recv()

        @pl.when(jnp.logical_and(g < z, z < last))
        def _():
            hop(g, ch, 1).start()

        @pl.when(jnp.logical_and(g > z, z > 0))
        def _():
            hop(g, ch, 0).start()

        share(g, ch).start()

    def arrivals(d, ch):
        @pl.when(z - d >= 0)
        def _():
            relay(z - d, ch)

        @pl.when(z + d <= last)
        def _():
            relay(z + d, ch)

        if ch == CHUNKS - 1:
            own = z_ref.at[piece(ch)]

            @pl.when(jnp.logical_and(d == last - 1, z == 1))
            def _():
                hop(z, ch, 0, own).start()

            @pl.when(jnp.logical_and(d == last - 1, z == last - 1))
            def _():
                hop(z, ch, 1, own).start()

    def f_copy(target, source):
        return pltpu.make_async_remote_copy(
            src_ref=f_sorted.at[target],
            dst_ref=f_all.at[source],
            send_sem=fsend.at[target],
            recv_sem=frecv.at[source],
            device_id=(target * PAIR + c, z),
            device_id_type=MESH,
        )

    f_load.wait()

    def sort_for(target, store):
        def one(s, carry):
            blocks = []
            for r in range(rows_here):
                t = scalars[r, target * each + s]
                block = f_raw[r, jnp.maximum(t, 0)]
                if slots > nz:
                    block = jnp.where(t >= 0, block, jnp.zeros_like(block))
                blocks.append(block)
            store(s, jnp.concatenate(blocks, axis=0).T)
            return carry

        lax.fori_loop(0, each, one, 0)

    for e in range(1, chips):
        target = peer(e)

        def to_send(s, tile):
            f_sorted[target, s] = tile

        sort_for(target, to_send)
        f_copy(target, q).start()

    def to_own(s, tile):
        f_all[q, s] = tile

    sort_for(q, to_own)

    z_load.wait()

    for ch in range(CHUNKS - 1):
        arrivals(1, ch)

    @pl.when(jnp.logical_and(z > 0, z < last))
    def _():
        arrivals(1, CHUNKS - 1)

    arrivals(2, 0)
    for e in range(1, chips):
        f_copy(q, peer(e)).wait_recv()

    fewer = jnp.minimum(z, last - z)
    more = jnp.where(z < last - z, 1, -1)

    def group_at(p):
        late = jnp.logical_and(jnp.logical_and(z > 0, z < last), p >= last - 1)
        p = jnp.where(late, 2 * last - 1 - p, p)
        near = jnp.where(p % 2 == 1, -more, more) * ((p + 1) // 2)
        far = more * (p - fewer)
        return z + jnp.where(p <= 2 * fewer, near, far)

    def s_copy(g, ch, slot, target, source):
        size = bounds[ch + 1] - bounds[ch]
        return pltpu.make_async_remote_copy(
            src_ref=s_send.at[slot, target, pl.ds(0, size)],
            dst_ref=s_all.at[g, ch, source, pl.ds(0, size)],
            send_sem=ssend.at[slot, target],
            recv_sem=srecv.at[g, ch, source],
            device_id=(target * PAIR + c, z),
            device_id_type=MESH,
        )

    def b_copy(g, s, target, source):
        return pltpu.make_async_remote_copy(
            src_ref=b_send.at[s, target],
            dst_ref=b_all.at[g, s, source],
            send_sem=bsend.at[s, target],
            recv_sem=brecv.at[g, s, source],
            device_id=(target, z),
            device_id_type=MESH,
        )

    def seat(e):
        return (k + e) % sites

    def c_copy(g, s, source):
        return pltpu.make_async_remote_copy(
            src_ref=c_send.at[g, s],
            dst_ref=c_all.at[s, source],
            send_sem=csend.at[g, s],
            recv_sem=crecv.at[s, source],
            device_id=(k, g),
            device_id_type=MESH,
        )

    beside = (1, last - 1)

    def is_end(plane):
        return jnp.logical_or(plane == 0, plane == last)

    def inner(plane):
        return jnp.logical_and(plane > 0, plane < last)

    def m_copy(end, s, source):
        return pltpu.make_async_remote_copy(
            src_ref=c_send.at[end * last, s],
            dst_ref=c_mid.at[end, s, source],
            send_sem=csend.at[end * last, s],
            recv_sem=mrecv.at[end, s, source],
            device_id=(k, beside[end]),
            device_id_type=MESH,
        )

    side = lax.broadcasted_iota(jnp.int32, (packed_rows, shared), 1) // share_of

    def pack(block, core):
        top, bottom = block[:packed_rows], block[hours - packed_rows :]
        if core:
            top = pltpu.roll(top, share_of, 1)
        else:
            bottom = pltpu.roll(bottom, share_of, 1)
        return jnp.where(side == 0, top, bottom)

    def multiply(g, ch, slot, kept):
        size = bounds[ch + 1] - bounds[ch]
        shared_in(g, ch).wait_recv()
        for half in range(PAIR):
            for b in range(held):
                z_work[half * held + b, 0:size, :] = z_all[
                    g, half, piece(ch), b * blk : (b + 1) * blk
                ]

        def product(i):
            total = None
            for s in range(each):
                term = lax.dot_general(
                    z_work[scalars[half_rows + i, s], 0:size, :],
                    f_all[i, s],
                    (((1,), (0,)), ((), ())),
                    preferred_element_type=jnp.float32,
                )
                total = term if total is None else total + term
            return total

        def one(e, carry):
            target = peer(e)
            s_send[slot, target, 0:size, :] = product(target).astype(s_send.dtype)
            s_copy(g, ch, slot, target, q).start()
            return carry

        lax.fori_loop(1, chips, one, 0)
        s_own[kept, 0:size, :] = product(q)

    def lane_of(p):
        return jnp.where(p == 1, 1, 0)

    def finish(p, ch, spare=False):
        g = group_at(p)
        size = bounds[ch + 1] - bounds[ch]
        total = s_own[CHUNKS if spare else ch, 0:size, :]
        for e in range(1, chips):
            s_copy(g, ch, 0, q, peer(e)).wait_recv()
            total = total + s_all[g, ch, peer(e), 0:size, :].astype(jnp.float32)
        s_sum[lane_of(p), bounds[ch] : bounds[ch + 1], :] = total
        for s in range(scens):
            if not bounds[ch] < (s + 1) * hours <= bounds[ch + 1]:
                continue
            spatial = s_sum[lane_of(p), s * hours : (s + 1) * hours, :].astype(jnp.bfloat16)
            weather = jnp.dot(temporal_ref[...], spatial, preferred_element_type=jnp.float32)
            spread = spread_ref[...]
            values = scale_ref[...] * jnp.exp(spread * weather - 0.5 * spread * spread)
            sums = lax.dot_general(
                values.astype(jnp.bfloat16),
                onehot[...],
                (((1,), (1,)), ((), ())),
                preferred_element_type=jnp.float32,
            )

            @pl.when(p > 0)
            def _():
                for e in range(1, sites):
                    b_copy(g, s, seat(e), k).wait_send()

            for i in range(chips):
                block = sums[:, i * shared : (i + 1) * shared]
                for core in range(PAIR):
                    b_send[s, i * PAIR + core] = pack(block, core).astype(b_send.dtype)
            for e in range(1, sites):
                b_copy(g, s, seat(e), k).start()
            b_all[g, s, k] = b_send[s, k]

    def forward(p, s):
        g = group_at(p)
        for e in range(1, sites):
            b_copy(g, s, k, seat(e)).wait_recv()
        total = b_all[g, s, 0].astype(jnp.float32)
        for i in range(1, sites):
            total = total + b_all[g, s, i].astype(jnp.float32)

        @pl.when(p == 0)
        def _():
            c_all[s, z] = total

        @pl.when(p > 0)
        def _():
            c_send[g, s] = total

            @pl.when(jnp.logical_or(is_end(z), inner(g)))
            def _():
                c_copy(g, s, z).start()

            for end, near in enumerate(beside):

                @pl.when(jnp.logical_and(inner(z), jnp.logical_and(g == end * last, z != near)))
                def _():
                    m_copy(end, s, z).start()

    def free(g, ch, slot):
        for e in range(1, chips):
            s_copy(g, ch, slot, peer(e), q).wait_send()

    def done_in(s):
        return next(ch for ch in range(CHUNKS) if (s + 1) * hours <= bounds[ch + 1])

    final = CHUNKS - 1

    def stage(p, ch, spare=False):
        g = group_at(p)

        @pl.when(p > 0)
        def _():
            free(g, ch, ch)

        multiply(g, ch, ch, CHUNKS if spare else ch)

    def position(p, carry):
        for ch in range(CHUNKS):
            if ch == final:

                @pl.when(jnp.logical_or(p != 1, inner(z)))
                def _():
                    stage(p, ch)

            else:
                stage(p, ch)
            for s in range(scens):
                at = done_in(s) + 3
                if at % CHUNKS == ch:
                    back = at // CHUNKS
                    ready = p >= back
                    if done_in(s) == final:
                        natural = jnp.logical_or(p != 1 + back, inner(z))
                        ready = jnp.logical_and(ready, natural)

                    @pl.when(ready)
                    def _():
                        forward(p - back, s)

            if ch > 0:
                finish(p, ch - 1)
            else:

                @pl.when(jnp.logical_and(p > 0, jnp.logical_or(p != 2, inner(z))))
                def _():
                    finish(p - 1, final)

            step = ch + 1
            if step < CHUNKS:

                @pl.when(p > 2)
                def _():
                    arrivals(p, step)
            else:

                @pl.when(jnp.logical_and(p >= 2, p < last))
                def _():
                    arrivals(p + 1, 0)

            for part in range(1, CHUNKS):
                if 2 * part % CHUNKS == ch:

                    @pl.when(p == 2 * part // CHUNKS)
                    def _():
                        arrivals(2, part)

        return carry

    lax.fori_loop(0, groups, position, 0)

    @pl.when(is_end(z))
    def _():
        arrivals(1, final)
        stage(1, final, True)

    finish(last, final)
    for s in range(scens):
        if done_in(s) < final and done_in(s) + 3 >= CHUNKS:
            forward(last, s)

    @pl.when(is_end(z))
    def _():
        finish(1, final, True)

    for s in range(scens):
        if done_in(s) == final:
            forward(last, s)

    @pl.when(is_end(z))
    def _():
        for s in range(scens):
            if done_in(s) == final:
                forward(1, s)

    for g in range(groups):
        for ch in range(CHUNKS):
            share(g, ch).wait_send()

            @pl.when(jnp.logical_and(g <= z, z < last))
            def _():
                hop(g, ch, 1).wait_send()

            @pl.when(jnp.logical_and(g >= z, z > 0))
            def _():
                hop(g, ch, 0).wait_send()

    for end, near in enumerate(beside):

        @pl.when(jnp.logical_and(inner(z), z == near))
        def _():
            for s in range(scens):
                total = c_send[end * last, s]
                for source in range(1, last):
                    if source != near:
                        m_copy(end, s, source).wait_recv()
                        total = total + c_mid[end, s, source]
                c_send[end * last, s] = total
                c_copy(end * last, s, z).start()

    def unpack(packed, s, ref):
        rest = pltpu.roll(packed[2 * packed_rows - hours :], share_of, 1)
        whole = jnp.concatenate([packed, rest], axis=0)
        ref[:, s * hours : (s + 1) * hours] = whole.T[:share_of]

    for s in range(scens):
        unpack(c_all[s, z], s, near_ref)
        c_sum[s] = jnp.zeros_like(c_sum[s])
    for s in range(scens):
        for d in range(1, groups):
            source = (z + d) % groups
            direct = jnp.logical_or(inner(z), is_end(source))
            for end, near in enumerate(beside):
                direct = jnp.logical_or(direct, jnp.logical_and(z == end * last, source == near))

            @pl.when(direct)
            def _():
                c_copy(z, s, source).wait_recv()
                c_sum[s] = c_sum[s] + c_all[s, source]

        unpack(c_sum[s], s, far_ref)

    for ch in range(CHUNKS):
        free(z, ch, ch)
    for e in range(1, chips):
        f_copy(peer(e), q).wait_send()
    for s in range(scens):
        for e in range(1, sites):
            b_copy(z, s, seat(e), k).wait_send()
    for s in range(scens):
        for d in range(1, groups):
            c_copy((z + d) % groups, s, z).wait_send()


def bounds_of(width):
    unit = width // 21
    return [0, 9 * unit, 18 * unit, width]


def shards(normals, pattern, factor, temporal, capacity, spread, bus_map, buses):
    sites = lax.axis_size("site")
    groups = lax.axis_size("scen")
    depth, width = normals.shape
    rows_here, nz, height, blk = factor.shape
    hours = temporal.shape[0]
    scens = width // hours
    chips = sites // PAIR
    bounds = bounds_of(width)
    step = max(b - a for a, b in zip(bounds, bounds[1:]))
    slots = sites * MAX_COLUMN_BLOCKS
    each = slots // chips
    rows = rows_here * height
    shared = buses // chips
    packed_rows = (hours // 2 + 7) // 8 * 8
    block_count = depth // blk
    lanes = -(-block_count * sites // LANES) * LANES
    half_rows = -(-max(chips, rows_here) // 8) * 8

    bf16, f32, i32 = jnp.bfloat16, jnp.float32, jnp.int32
    dma = pltpu.SemaphoreType.DMA
    whole = pl.BlockSpec(memory_space=pltpu.VMEM)
    anywhere = pl.BlockSpec(memory_space=pltpu.HBM)
    scratch = [
        pltpu.VMEM(pattern.shape, i32),
        pltpu.VMEM(temporal.shape, bf16),
        pltpu.VMEM((capacity.size // LANES, LANES), f32),
        pltpu.VMEM((spread.size // LANES, LANES), f32),
        pltpu.VMEM((bus_map.size // LANES, LANES), i32),
        pltpu.VMEM((groups, PAIR, width, depth), bf16),
        pltpu.VMEM((PAIR * block_count, step, blk), bf16),
        pltpu.VMEM((rows_here, nz, height, blk), bf16),
        pltpu.VMEM((chips, each, blk, rows), bf16),
        pltpu.VMEM((chips, each, blk, rows), bf16),
        pltpu.VMEM((CHUNKS, chips, step, rows), bf16),
        pltpu.VMEM((CHUNKS + 1, step, rows), f32),
        pltpu.VMEM((groups, CHUNKS, chips, step, rows), bf16),
        pltpu.VMEM((2, width, rows), f32),
        pltpu.VMEM((scens, sites, packed_rows, shared), bf16),
        pltpu.VMEM((groups, scens, sites, packed_rows, shared), bf16),
        pltpu.VMEM((groups, scens, packed_rows, shared), f32),
        pltpu.VMEM((scens, groups, packed_rows, shared), f32),
        pltpu.VMEM((2, scens, groups, packed_rows, shared), f32),
        pltpu.VMEM((scens, packed_rows, shared), f32),
        pltpu.VMEM((buses, rows), bf16),
        pltpu.VMEM((1, rows), f32),
        pltpu.VMEM((1, rows), f32),
        pltpu.VMEM((pattern.shape[0], lanes), i32),
        pltpu.VMEM((sites, lanes), i32),
        pltpu.VMEM((sites, lanes), i32),
        pltpu.VMEM((3, half_rows, lanes), i32),
        pltpu.VMEM((2 * half_rows, LANES), i32),
        pltpu.SMEM((2 * half_rows, LANES), i32),
        dma((8,)),
        dma((2, groups, CHUNKS)),
        dma((groups, CHUNKS)),
        dma((groups, CHUNKS)),
        dma((groups, CHUNKS)),
        dma((chips,)),
        dma((chips,)),
        dma((CHUNKS, chips)),
        dma((groups, CHUNKS, chips)),
        dma((scens, sites)),
        dma((groups, scens, sites)),
        dma((groups, scens)),
        dma((scens, groups)),
        dma((2, scens, groups)),
        pltpu.SemaphoreType.REGULAR((max(chips.bit_length() - 2, 1),)),
    ]
    taken = sum(
        math.prod(ref.shape) * ref.dtype.itemsize
        for ref in scratch
        if ref.memory_space == pltpu.VMEM
    )
    limit = min(taken + taken // 16 + VMEM_MARGIN, VMEM_LIMIT)
    near, far = pl.pallas_call(
        functools.partial(kernel, chips, groups, slots, hours),
        out_shape=[jax.ShapeDtypeStruct((buses // sites, width), f32)] * 2,
        in_specs=[anywhere] * 7,
        out_specs=[whole] * 2,
        scratch_shapes=scratch,
        compiler_params=pltpu.CompilerParams(
            collective_id=0, has_side_effects=True, vmem_limit_bytes=limit
        ),
    )(
        *(
            pltpu.with_memory_space_constraint(x, pltpu.HBM)
            for x in (
                pattern,
                normals.T,
                factor,
                temporal,
                capacity.reshape(-1, LANES),
                spread.reshape(-1, LANES),
                bus_map.reshape(-1, LANES),
            )
        )
    )
    return near + far


def solution(mesh):
    placed = (P("site", "scen"), P(), P("site", None, "scen", None), P(), P("site"), P("site"), P())
    sites = mesh.shape["site"]

    def whole(normals, pattern, factor, temporal, capacity, spread, bus_map):
        buses = factor.shape[0] * factor.shape[3] // 16

        def body(*args):
            return shards(*args, buses)

        return jax.shard_map(
            body, mesh=mesh, in_specs=placed, out_specs=P("site", "scen"), check_vma=False
        )(normals, pattern, factor, temporal, capacity, spread, bus_map)

    return whole
```

```python
import functools
import math

import jax
import jax.numpy as jnp
from jax import lax
from jax.experimental import pallas as pl
from jax.experimental.pallas import tpu as pltpu
from jax.sharding import PartitionSpec as P

MAX_COLUMN_BLOCKS = 5
PAIR = 2
CHUNKS = 3
LANES = 128
VMEM_LIMIT = 67043328
VMEM_MARGIN = 3 * 1024 * 1024
MESH = pl.DeviceIdType.MESH


def kernel(
    chips,
    groups,
    slots,
    hours,
    pattern_hbm,
    z_ref,
    f_ref,
    temporal_hbm,
    capacity_hbm,
    spreads_hbm,
    buses_hbm,
    near_ref,
    far_ref,
    pattern_ref,
    temporal_ref,
    capacity_ref,
    spreads_ref,
    buses_ref,
    z_all,
    z_work,
    f_raw,
    f_sorted,
    f_all,
    s_send,
    s_own,
    s_all,
    s_sum,
    b_send,
    b_all,
    c_send,
    c_all,
    c_mid,
    c_sum,
    onehot,
    scale_ref,
    spread_ref,
    pos,
    need,
    ranks,
    gathered,
    tables,
    scalars,
    local_sem,
    zsend,
    zrecv,
    psend,
    precv,
    fsend,
    frecv,
    ssend,
    srecv,
    bsend,
    brecv,
    csend,
    crecv,
    mrecv,
    meet,
):
    k = lax.axis_index("site")
    z = lax.axis_index("scen")
    q = k // PAIR
    c = k % PAIR
    other = q * PAIR + (PAIR - 1 - c)
    rows_here, nz, height, blk = f_ref.shape
    width, depth = z_ref.shape
    bounds = bounds_of(width)
    each = slots // chips
    scens = width // hours
    share_of = near_ref.shape[0]
    shared = share_of * PAIR
    packed_rows = b_send.shape[2]
    sites = chips * PAIR
    held = depth // blk
    lanes = pos.shape[1]
    rows = rows_here * height
    last = groups - 1

    bits = [1 << i for i in range(chips.bit_length() - 1)]

    def across(bit):
        return q + bit - 2 * bit * ((q // bit) % 2)

    barrier = pltpu.get_barrier_semaphore()

    def flip(i, mask, count):
        total, bit = 0, 1
        while bit < count:
            a, b = (i // bit) % 2, (mask // bit) % 2
            total = total + bit * (a + b - 2 * a * b)
            bit *= 2
        return total

    def peer(e):
        return flip(q, chips - e, chips)

    def greet(device):
        pl.semaphore_signal(barrier, inc=1, device_id=device, device_id_type=MESH)

    @pl.when(z < last)
    def _():
        greet((k, z + 1))

    @pl.when(z > 0)
    def _():
        greet((k, z - 1))

    greet((other, z))
    for bit in bits:
        greet((across(bit) * PAIR + c, z))

    small = [
        (pattern_hbm, pattern_ref),
        (temporal_hbm, temporal_ref),
        (capacity_hbm, capacity_ref),
        (spreads_hbm, spreads_ref),
        (buses_hbm, buses_ref),
    ]
    loads = [
        pltpu.make_async_copy(source, target, local_sem.at[3 + i])
        for i, (source, target) in enumerate(small)
    ]
    for load in loads:
        load.start()
    z_load = pltpu.make_async_copy(z_ref, z_all.at[z, c], local_sem.at[0])
    z_load.start()
    f_load = pltpu.make_async_copy(f_ref, f_raw, local_sem.at[1])
    f_load.start()
    for load in loads:
        load.wait()

    lane = lax.broadcasted_iota(jnp.int32, (1, lanes), 1)
    owner = jnp.zeros_like(lane)
    for j in range(1, sites):
        owner = owner + jnp.where(lane >= j * held, 1, 0)
    local = lane - owner * held
    found = jnp.zeros(pos.shape, jnp.int32)
    for t in range(nz):
        found = jnp.where(pattern_ref[:, t : t + 1] == lane, t + 1, found)
    pos[...] = found
    for i in range(sites):
        line = pos[i * rows_here : i * rows_here + 1, :]
        for r in range(1, rows_here):
            at = i * rows_here + r
            line = jnp.maximum(line, pos[at : at + 1, :])
        need[i : i + 1, :] = jnp.where(line > 0, 1, 0)
    wanted = need[...]
    before = jnp.zeros_like(wanted)
    for d in range(1, held):
        before = before + jnp.where(local >= d, pltpu.roll(wanted, d, 1), 0)
    ranks[...] = before

    half_rows = tables.shape[0] // 2
    column = lax.broadcasted_iota(jnp.int32, (half_rows, tables.shape[1]), 1)
    gathered[...] = jnp.zeros_like(gathered)
    for r in range(rows_here):
        gathered[0, r : r + 1, :] = pos[pl.ds(k * rows_here + r, 1), :]
    for i in range(chips):
        gathered[1, i : i + 1, :] = need[pl.ds(i * PAIR + c, 1), :]
        gathered[2, i : i + 1, :] = ranks[pl.ds(i * PAIR + c, 1), :]
    own_slot = owner * MAX_COLUMN_BLOCKS + ranks[pl.ds(k, 1), :]
    own_slot = jnp.where(need[pl.ds(k, 1), :] > 0, own_slot, -1)
    places = jnp.zeros(column.shape, jnp.int32)
    positions = gathered[0]
    for t in range(slots):
        at = jnp.sum(jnp.where(own_slot == t, positions, 0), axis=1, keepdims=True)
        places = jnp.where(column == t, at, places)
    tables[0:half_rows, :] = places - 1
    blocks = jnp.zeros(column.shape, jnp.int32)
    needs, orders = gathered[1], gathered[2]
    first = q * PAIR * held
    for half in range(PAIR):
        mine = jnp.where(owner == q * PAIR + half, needs, 0)
        for j in range(MAX_COLUMN_BLOCKS):
            hit = jnp.where(orders == j, mine, 0)
            at = jnp.sum(hit * (lane - first), axis=1, keepdims=True)
            blocks = jnp.where(column == half * MAX_COLUMN_BLOCKS + j, at, blocks)
    tables[half_rows:, :] = blocks
    t_load = pltpu.make_async_copy(tables, scalars, local_sem.at[2])
    t_load.start()

    ends = jnp.where(z < last, 1, 0) + jnp.where(z > 0, 1, 0)
    pl.semaphore_wait(barrier, 1 + len(bits) + ends)

    def piece(ch):
        return pl.ds(bounds[ch], bounds[ch + 1] - bounds[ch])

    def hop(g, ch, up, source=None):
        part = z_all.at[g, c, piece(ch)]
        return pltpu.make_async_remote_copy(
            src_ref=part if source is None else source,
            dst_ref=part,
            send_sem=zsend.at[up, g, ch],
            recv_sem=zrecv.at[g, ch],
            device_id=(k, z + 1 if up else z - 1),
            device_id_type=MESH,
        )

    def share(g, ch, source=None):
        part = z_all.at[g, c, piece(ch)]
        return pltpu.make_async_remote_copy(
            src_ref=part if source is None else source,
            dst_ref=part,
            send_sem=psend.at[g, ch],
            recv_sem=precv.at[g, ch],
            device_id=(other, z),
            device_id_type=MESH,
        )

    def came_in(g, ch):
        part = z_all.at[g, c, piece(ch)]
        return pltpu.make_async_remote_copy(
            src_ref=part,
            dst_ref=part,
            send_sem=psend.at[g, ch],
            recv_sem=zrecv.at[g, ch],
            device_id=(other, z),
            device_id_type=MESH,
        )

    def shared_in(g, ch):
        part = z_all.at[g, 1 - c, piece(ch)]
        return pltpu.make_async_remote_copy(
            src_ref=part,
            dst_ref=part,
            send_sem=psend.at[g, ch],
            recv_sem=precv.at[g, ch],
            device_id=(other, z),
            device_id_type=MESH,
        )

    for ch in range(CHUNKS):
        own = z_ref.at[piece(ch)]
        late = ch == CHUNKS - 1

        @pl.when(z < (last - 1 if late else last))
        def _():
            hop(z, ch, 1, own).start()

        @pl.when(z > (1 if late else 0))
        def _():
            hop(z, ch, 0, own).start()

    for ch in range(CHUNKS):
        share(z, ch, z_ref.at[piece(ch)]).start()

    for i, bit in enumerate(bits[:-1]):
        pl.semaphore_signal(
            meet.at[i], inc=1, device_id=(across(bit) * PAIR + c, z), device_id_type=MESH
        )
        pl.semaphore_wait(meet.at[i], 1)


    narrow = capacity_ref.shape[1]
    narrow_lane = lax.broadcasted_iota(jnp.int32, (8, narrow), 1)
    offset = z * height

    def rows_of(ref, base):
        parts = []
        for start in range(0, rows, narrow):
            part = None
            for r in range(start // height, min((start + narrow) // height, rows_here)):
                line = ref[pl.ds(base + r * blk // narrow + offset // narrow, 1), :]
                line = jnp.broadcast_to(line, narrow_lane.shape)
                shift = (r * height - start + narrow - offset % narrow) % narrow
                line = pltpu.roll(line, shift, 1)
                if part is None:
                    part = line
                else:
                    part = jnp.where(narrow_lane >= r * height - start, line, part)
            parts.append(part[0:1])
        return jnp.concatenate(parts, axis=1) if len(parts) > 1 else parts[0]

    scale_ref[...] = rows_of(capacity_ref, 0)
    spread_ref[...] = rows_of(spreads_ref, 0)
    maps = rows_of(buses_ref, k * (rows_here * blk // narrow))
    bus_ids = lax.broadcasted_iota(jnp.int32, onehot.shape, 0)
    onehot[...] = jnp.where(bus_ids == maps, 1.0, 0.0).astype(onehot.dtype)
    t_load.wait()

    def relay(g, ch):
        came_in(g, ch).wait_recv()

        @pl.when(jnp.logical_and(g < z, z < last))
        def _():
            hop(g, ch, 1).start()

        @pl.when(jnp.logical_and(g > z, z > 0))
        def _():
            hop(g, ch, 0).start()

        share(g, ch).start()

    def arrivals(d, ch):
        @pl.when(z - d >= 0)
        def _():
            relay(z - d, ch)

        @pl.when(z + d <= last)
        def _():
            relay(z + d, ch)

        if ch == CHUNKS - 1:
            own = z_ref.at[piece(ch)]

            @pl.when(jnp.logical_and(d == last - 1, z == 1))
            def _():
                hop(z, ch, 0, own).start()

            @pl.when(jnp.logical_and(d == last - 1, z == last - 1))
            def _():
                hop(z, ch, 1, own).start()

    def f_copy(target, source):
        return pltpu.make_async_remote_copy(
            src_ref=f_sorted.at[target],
            dst_ref=f_all.at[source],
            send_sem=fsend.at[target],
            recv_sem=frecv.at[source],
            device_id=(target * PAIR + c, z),
            device_id_type=MESH,
        )

    f_load.wait()

    def sort_for(target, store):
        def one(s, carry):
            blocks = []
            for r in range(rows_here):
                t = scalars[r, target * each + s]
                block = f_raw[r, jnp.maximum(t, 0)]
                if slots > nz:
                    block = jnp.where(t >= 0, block, jnp.zeros_like(block))
                blocks.append(block)
            store(s, jnp.concatenate(blocks, axis=0).T)
            return carry

        lax.fori_loop(0, each, one, 0)

    for e in range(1, chips):
        target = peer(e)

        def to_send(s, tile):
            f_sorted[target, s] = tile

        sort_for(target, to_send)
        f_copy(target, q).start()

    def to_own(s, tile):
        f_all[q, s] = tile

    sort_for(q, to_own)

    z_load.wait()

    for ch in range(CHUNKS - 1):
        arrivals(1, ch)

    @pl.when(jnp.logical_and(z > 0, z < last))
    def _():
        arrivals(1, CHUNKS - 1)

    arrivals(2, 0)
    for e in range(1, chips):
        f_copy(q, peer(e)).wait_recv()

    fewer = jnp.minimum(z, last - z)
    more = jnp.where(z < last - z, 1, -1)

    def group_at(p):
        late = jnp.logical_and(jnp.logical_and(z > 0, z < last), p >= last - 1)
        p = jnp.where(late, 2 * last - 1 - p, p)
        near = jnp.where(p % 2 == 1, -more, more) * ((p + 1) // 2)
        far = more * (p - fewer)
        return z + jnp.where(p <= 2 * fewer, near, far)

    def s_copy(g, ch, slot, target, source):
        size = bounds[ch + 1] - bounds[ch]
        return pltpu.make_async_remote_copy(
            src_ref=s_send.at[slot, target, pl.ds(0, size)],
            dst_ref=s_all.at[g, ch, source, pl.ds(0, size)],
            send_sem=ssend.at[slot, target],
            recv_sem=srecv.at[g, ch, source],
            device_id=(target * PAIR + c, z),
            device_id_type=MESH,
        )

    def b_copy(g, s, target, source, slot=None):
        slot = s if slot is None else slot
        return pltpu.make_async_remote_copy(
            src_ref=b_send.at[slot, target],
            dst_ref=b_all.at[g, s, source],
            send_sem=bsend.at[slot, target],
            recv_sem=brecv.at[g, s, source],
            device_id=(target, z),
            device_id_type=MESH,
        )

    def seat(e):
        return flip(k, sites - e, sites)

    def c_copy(g, s, source):
        return pltpu.make_async_remote_copy(
            src_ref=c_send.at[g, s],
            dst_ref=c_all.at[s, source],
            send_sem=csend.at[g, s],
            recv_sem=crecv.at[s, source],
            device_id=(k, g),
            device_id_type=MESH,
        )

    beside = (1, last - 1)

    def is_end(plane):
        return jnp.logical_or(plane == 0, plane == last)

    def inner(plane):
        return jnp.logical_and(plane > 0, plane < last)

    def m_copy(end, s, source):
        return pltpu.make_async_remote_copy(
            src_ref=c_send.at[end * last, s],
            dst_ref=c_mid.at[end, s, source],
            send_sem=csend.at[end * last, s],
            recv_sem=mrecv.at[end, s, source],
            device_id=(k, beside[end]),
            device_id_type=MESH,
        )

    side = lax.broadcasted_iota(jnp.int32, (packed_rows, shared), 1) // share_of

    def pack(block, core):
        top, bottom = block[:packed_rows], block[hours - packed_rows :]
        if core:
            top = pltpu.roll(top, share_of, 1)
        else:
            bottom = pltpu.roll(bottom, share_of, 1)
        return jnp.where(side == 0, top, bottom)

    def multiply(g, ch, slot, kept):
        size = bounds[ch + 1] - bounds[ch]
        shared_in(g, ch).wait_recv()
        for half in range(PAIR):
            for b in range(held):
                z_work[half * held + b, 0:size, :] = z_all[
                    g, half, piece(ch), b * blk : (b + 1) * blk
                ]

        def product(i):
            total = None
            for s in range(each):
                term = lax.dot_general(
                    z_work[scalars[half_rows + i, s], 0:size, :],
                    f_all[i, s],
                    (((1,), (0,)), ((), ())),
                    preferred_element_type=jnp.float32,
                )
                total = term if total is None else total + term
            return total

        def one(e, carry):
            target = peer(e)
            s_send[slot, target, 0:size, :] = product(target).astype(s_send.dtype)
            s_copy(g, ch, slot, target, q).start()
            return carry

        lax.fori_loop(1, chips, one, 0)
        s_own[kept, 0:size, :] = product(q)

    def lane_of(p):
        return jnp.where(p == 1, 1, 0)

    def finish(p, ch, spare=False):
        g = group_at(p)
        size = bounds[ch + 1] - bounds[ch]
        total = s_own[CHUNKS if spare else ch, 0:size, :]
        for e in range(1, chips):
            s_copy(g, ch, 0, q, peer(e)).wait_recv()
            total = total + s_all[g, ch, peer(e), 0:size, :].astype(jnp.float32)
        s_sum[lane_of(p), bounds[ch] : bounds[ch + 1], :] = total
        for s in range(scens):
            if not bounds[ch] < (s + 1) * hours <= bounds[ch + 1]:
                continue
            spatial = s_sum[lane_of(p), s * hours : (s + 1) * hours, :].astype(jnp.bfloat16)
            weather = jnp.dot(temporal_ref[...], spatial, preferred_element_type=jnp.float32)
            spread = spread_ref[...]
            values = scale_ref[...] * jnp.exp(spread * weather - 0.5 * spread * spread)
            sums = lax.dot_general(
                values.astype(jnp.bfloat16),
                onehot[...],
                (((1,), (1,)), ((), ())),
                preferred_element_type=jnp.float32,
            )

            slot = scens if spare else s
            if not spare:

                @pl.when(p > 0)
                def _():
                    for e in range(1, sites):
                        b_copy(g, s, seat(e), k).wait_send()

            for i in range(chips):
                block = sums[:, i * shared : (i + 1) * shared]
                for core in range(PAIR):
                    b_send[slot, i * PAIR + core] = pack(block, core).astype(b_send.dtype)
            for e in range(1, sites):
                b_copy(g, s, seat(e), k, slot).start()
            b_all[g, s, k] = b_send[slot, k]

    def forward(p, s):
        g = group_at(p)
        for e in range(1, sites):
            b_copy(g, s, k, seat(e)).wait_recv()
        total = b_all[g, s, 0].astype(jnp.float32)
        for i in range(1, sites):
            total = total + b_all[g, s, i].astype(jnp.float32)

        @pl.when(p == 0)
        def _():
            c_all[s, z] = total

        @pl.when(p > 0)
        def _():
            c_send[g, s] = total

            @pl.when(jnp.logical_or(is_end(z), inner(g)))
            def _():
                c_copy(g, s, z).start()

            for end, near in enumerate(beside):

                @pl.when(jnp.logical_and(inner(z), jnp.logical_and(g == end * last, z != near)))
                def _():
                    m_copy(end, s, z).start()

    def free(g, ch, slot):
        for e in range(1, chips):
            s_copy(g, ch, slot, peer(e), q).wait_send()

    def done_in(s):
        return next(ch for ch in range(CHUNKS) if (s + 1) * hours <= bounds[ch + 1])

    final = CHUNKS - 1

    def stage(p, ch, spare=False):
        g = group_at(p)

        @pl.when(p > 0)
        def _():
            free(g, ch, ch)

        multiply(g, ch, ch, CHUNKS if spare else ch)

    def position(p, carry):
        for ch in range(CHUNKS):
            if ch == final:

                @pl.when(jnp.logical_or(p != 1, inner(z)))
                def _():
                    stage(p, ch)

            else:
                stage(p, ch)
            for s in range(scens):
                at = done_in(s) + 3
                if at % CHUNKS == ch:
                    back = at // CHUNKS
                    ready = p >= back
                    if done_in(s) == final:
                        natural = jnp.logical_or(p != 1 + back, inner(z))
                        ready = jnp.logical_and(ready, natural)

                    @pl.when(ready)
                    def _():
                        forward(p - back, s)

            if ch > 0:
                finish(p, ch - 1)
            else:

                @pl.when(jnp.logical_and(p > 0, jnp.logical_or(p != 2, inner(z))))
                def _():
                    finish(p - 1, final)

            step = ch + 1
            if step < CHUNKS:

                @pl.when(p > 2)
                def _():
                    arrivals(p, step)
            else:

                @pl.when(jnp.logical_and(p >= 2, p < last))
                def _():
                    arrivals(p + 1, 0)

            for part in range(1, CHUNKS):
                if 2 * part % CHUNKS == ch:

                    @pl.when(p == 2 * part // CHUNKS)
                    def _():
                        arrivals(2, part)

        return carry

    lax.fori_loop(0, groups, position, 0)

    @pl.when(is_end(z))
    def _():
        arrivals(1, final)
        stage(1, final, True)

    finish(last, final)
    for s in range(scens):
        if done_in(s) < final and done_in(s) + 3 >= CHUNKS:
            forward(last, s)

    @pl.when(is_end(z))
    def _():
        finish(1, final, True)

    for s in range(scens):
        if done_in(s) == final:
            forward(last, s)

    @pl.when(is_end(z))
    def _():
        for s in range(scens):
            if done_in(s) == final:
                forward(1, s)

    for g in range(groups):
        for ch in range(CHUNKS):
            share(g, ch).wait_send()

            @pl.when(jnp.logical_and(g <= z, z < last))
            def _():
                hop(g, ch, 1).wait_send()

            @pl.when(jnp.logical_and(g >= z, z > 0))
            def _():
                hop(g, ch, 0).wait_send()

    for end, near in enumerate(beside):

        @pl.when(jnp.logical_and(inner(z), z == near))
        def _():
            for s in range(scens):
                total = c_send[end * last, s]
                for source in range(1, last):
                    if source != near:
                        m_copy(end, s, source).wait_recv()
                        total = total + c_mid[end, s, source]
                c_send[end * last, s] = total
                c_copy(end * last, s, z).start()

    def unpack(packed, s, ref):
        rest = pltpu.roll(packed[2 * packed_rows - hours :], share_of, 1)
        whole = jnp.concatenate([packed, rest], axis=0)
        ref[:, s * hours : (s + 1) * hours] = whole.T[:share_of]

    for s in range(scens):
        unpack(c_all[s, z], s, near_ref)
        c_sum[s] = jnp.zeros_like(c_sum[s])
    for s in range(scens):
        for d in range(1, groups):
            source = (z + d) % groups
            direct = jnp.logical_or(inner(z), is_end(source))
            for end, near in enumerate(beside):
                direct = jnp.logical_or(direct, jnp.logical_and(z == end * last, source == near))

            @pl.when(direct)
            def _():
                c_copy(z, s, source).wait_recv()
                c_sum[s] = c_sum[s] + c_all[s, source]

        unpack(c_sum[s], s, far_ref)

    for ch in range(CHUNKS):
        free(z, ch, ch)
    for e in range(1, chips):
        f_copy(peer(e), q).wait_send()
    for s in range(scens):
        for e in range(1, sites):
            b_copy(z, s, seat(e), k).wait_send()

    @pl.when(is_end(z))
    def _():
        for e in range(1, sites):
            b_copy(z, 0, seat(e), k, scens).wait_send()

    for s in range(scens):
        for d in range(1, groups):
            c_copy((z + d) % groups, s, z).wait_send()


def bounds_of(width):
    unit = width // 21
    return [0, 9 * unit, 18 * unit, width]


def shards(normals, pattern, factor, temporal, capacity, spread, bus_map, buses):
    sites = lax.axis_size("site")
    groups = lax.axis_size("scen")
    depth, width = normals.shape
    rows_here, nz, height, blk = factor.shape
    hours = temporal.shape[0]
    scens = width // hours
    chips = sites // PAIR
    bounds = bounds_of(width)
    step = max(b - a for a, b in zip(bounds, bounds[1:]))
    slots = sites * MAX_COLUMN_BLOCKS
    each = slots // chips
    rows = rows_here * height
    shared = buses // chips
    packed_rows = (hours // 2 + 7) // 8 * 8
    block_count = depth // blk
    lanes = -(-block_count * sites // LANES) * LANES
    half_rows = -(-max(chips, rows_here) // 8) * 8

    bf16, f32, i32 = jnp.bfloat16, jnp.float32, jnp.int32
    dma = pltpu.SemaphoreType.DMA
    whole = pl.BlockSpec(memory_space=pltpu.VMEM)
    anywhere = pl.BlockSpec(memory_space=pltpu.HBM)
    scratch = [
        pltpu.VMEM(pattern.shape, i32),
        pltpu.VMEM(temporal.shape, bf16),
        pltpu.VMEM((capacity.size // LANES, LANES), f32),
        pltpu.VMEM((spread.size // LANES, LANES), f32),
        pltpu.VMEM((bus_map.size // LANES, LANES), i32),
        pltpu.VMEM((groups, PAIR, width, depth), bf16),
        pltpu.VMEM((PAIR * block_count, step, blk), bf16),
        pltpu.VMEM((rows_here, nz, height, blk), bf16),
        pltpu.VMEM((chips, each, blk, rows), bf16),
        pltpu.VMEM((chips, each, blk, rows), bf16),
        pltpu.VMEM((CHUNKS, chips, step, rows), bf16),
        pltpu.VMEM((CHUNKS + 1, step, rows), f32),
        pltpu.VMEM((groups, CHUNKS, chips, step, rows), bf16),
        pltpu.VMEM((2, width, rows), f32),
        pltpu.VMEM((scens + 1, sites, packed_rows, shared), bf16),
        pltpu.VMEM((groups, scens, sites, packed_rows, shared), bf16),
        pltpu.VMEM((groups, scens, packed_rows, shared), f32),
        pltpu.VMEM((scens, groups, packed_rows, shared), f32),
        pltpu.VMEM((2, scens, groups, packed_rows, shared), f32),
        pltpu.VMEM((scens, packed_rows, shared), f32),
        pltpu.VMEM((buses, rows), bf16),
        pltpu.VMEM((1, rows), f32),
        pltpu.VMEM((1, rows), f32),
        pltpu.VMEM((pattern.shape[0], lanes), i32),
        pltpu.VMEM((sites, lanes), i32),
        pltpu.VMEM((sites, lanes), i32),
        pltpu.VMEM((3, half_rows, lanes), i32),
        pltpu.VMEM((2 * half_rows, LANES), i32),
        pltpu.SMEM((2 * half_rows, LANES), i32),
        dma((8,)),
        dma((2, groups, CHUNKS)),
        dma((groups, CHUNKS)),
        dma((groups, CHUNKS)),
        dma((groups, CHUNKS)),
        dma((chips,)),
        dma((chips,)),
        dma((CHUNKS, chips)),
        dma((groups, CHUNKS, chips)),
        dma((scens + 1, sites)),
        dma((groups, scens, sites)),
        dma((groups, scens)),
        dma((scens, groups)),
        dma((2, scens, groups)),
        pltpu.SemaphoreType.REGULAR((max(chips.bit_length() - 2, 1),)),
    ]
    taken = sum(
        math.prod(ref.shape) * ref.dtype.itemsize
        for ref in scratch
        if ref.memory_space == pltpu.VMEM
    )
    limit = min(taken + taken // 16 + VMEM_MARGIN, VMEM_LIMIT)
    near, far = pl.pallas_call(
        functools.partial(kernel, chips, groups, slots, hours),
        out_shape=[jax.ShapeDtypeStruct((buses // sites, width), f32)] * 2,
        in_specs=[anywhere] * 7,
        out_specs=[whole] * 2,
        scratch_shapes=scratch,
        compiler_params=pltpu.CompilerParams(
            collective_id=0, has_side_effects=True, vmem_limit_bytes=limit
        ),
    )(
        *(
            pltpu.with_memory_space_constraint(x, pltpu.HBM)
            for x in (
                pattern,
                normals.T,
                factor,
                temporal,
                capacity.reshape(-1, LANES),
                spread.reshape(-1, LANES),
                bus_map.reshape(-1, LANES),
            )
        )
    )
    return near + far


def solution(mesh):
    placed = (P("site", "scen"), P(), P("site", None, "scen", None), P(), P("site"), P("site"), P())
    sites = mesh.shape["site"]

    def whole(normals, pattern, factor, temporal, capacity, spread, bus_map):
        buses = factor.shape[0] * factor.shape[3] // 16

        def body(*args):
            return shards(*args, buses)

        return jax.shard_map(
            body, mesh=mesh, in_specs=placed, out_specs=P("site", "scen"), check_vma=False
        )(normals, pattern, factor, temporal, capacity, spread, bus_map)

    return whole
```

```python
import functools
import math

import jax
import jax.numpy as jnp
from jax import lax
from jax.experimental import pallas as pl
from jax.experimental.pallas import tpu as pltpu
from jax.sharding import PartitionSpec as P

MAX_COLUMN_BLOCKS = 5
PAIR = 2
CHUNKS = 3
LANES = 128
VMEM_LIMIT = 67043328
VMEM_MARGIN = 3 * 1024 * 1024
MESH = pl.DeviceIdType.MESH


def kernel(
    chips,
    groups,
    slots,
    hours,
    pattern_hbm,
    z_ref,
    f_ref,
    temporal_hbm,
    capacity_hbm,
    spreads_hbm,
    buses_hbm,
    near_ref,
    far_ref,
    pattern_ref,
    temporal_ref,
    capacity_ref,
    spreads_ref,
    buses_ref,
    z_all,
    z_work,
    f_raw,
    f_sorted,
    f_all,
    s_send,
    s_own,
    s_all,
    s_sum,
    b_send,
    b_all,
    c_send,
    c_all,
    c_mid,
    c_sum,
    onehot,
    scale_ref,
    spread_ref,
    pos,
    need,
    ranks,
    gathered,
    tables,
    scalars,
    local_sem,
    zsend,
    zrecv,
    psend,
    precv,
    fsend,
    frecv,
    ssend,
    srecv,
    bsend,
    brecv,
    csend,
    crecv,
    mrecv,
    meet,
):
    k = lax.axis_index("site")
    z = lax.axis_index("scen")
    q = k // PAIR
    c = k % PAIR
    other = q * PAIR + (PAIR - 1 - c)
    rows_here, nz, height, blk = f_ref.shape
    width, depth = z_ref.shape
    bounds = bounds_of(width)
    each = slots // chips
    scens = width // hours
    share_of = near_ref.shape[0]
    shared = share_of * PAIR
    packed_rows = b_send.shape[2]
    sites = chips * PAIR
    held = depth // blk
    lanes = pos.shape[1]
    rows = rows_here * height
    last = groups - 1

    bits = [1 << i for i in range(chips.bit_length() - 1)]

    def across(bit):
        return q + bit - 2 * bit * ((q // bit) % 2)

    barrier = pltpu.get_barrier_semaphore()

    def flip(i, mask, count):
        total, bit = 0, 1
        while bit < count:
            a, b = (i // bit) % 2, (mask // bit) % 2
            total = total + bit * (a + b - 2 * a * b)
            bit *= 2
        return total

    def peer(e):
        return flip(q, chips - e, chips)

    def greet(device):
        pl.semaphore_signal(barrier, inc=1, device_id=device, device_id_type=MESH)

    @pl.when(z < last)
    def _():
        greet((k, z + 1))

    @pl.when(z > 0)
    def _():
        greet((k, z - 1))

    greet((other, z))
    for bit in bits:
        greet((across(bit) * PAIR + c, z))

    small = [
        (pattern_hbm, pattern_ref),
        (temporal_hbm, temporal_ref),
        (capacity_hbm, capacity_ref),
        (spreads_hbm, spreads_ref),
        (buses_hbm, buses_ref),
    ]
    loads = [
        pltpu.make_async_copy(source, target, local_sem.at[3 + i])
        for i, (source, target) in enumerate(small)
    ]
    for load in loads:
        load.start()
    ends = jnp.where(z < last, 1, 0) + jnp.where(z > 0, 1, 0)
    pl.semaphore_wait(barrier, 1 + len(bits) + ends)

    def piece(ch):
        return pl.ds(bounds[ch], bounds[ch + 1] - bounds[ch])

    def hop(g, ch, up, source=None):
        part = z_all.at[g, c, piece(ch)]
        return pltpu.make_async_remote_copy(
            src_ref=part if source is None else source,
            dst_ref=part,
            send_sem=zsend.at[up, g, ch],
            recv_sem=zrecv.at[g, ch],
            device_id=(k, z + 1 if up else z - 1),
            device_id_type=MESH,
        )

    def share(g, ch, source=None):
        part = z_all.at[g, c, piece(ch)]
        return pltpu.make_async_remote_copy(
            src_ref=part if source is None else source,
            dst_ref=part,
            send_sem=psend.at[g, ch],
            recv_sem=precv.at[g, ch],
            device_id=(other, z),
            device_id_type=MESH,
        )

    def came_in(g, ch):
        part = z_all.at[g, c, piece(ch)]
        return pltpu.make_async_remote_copy(
            src_ref=part,
            dst_ref=part,
            send_sem=psend.at[g, ch],
            recv_sem=zrecv.at[g, ch],
            device_id=(other, z),
            device_id_type=MESH,
        )

    def shared_in(g, ch):
        part = z_all.at[g, 1 - c, piece(ch)]
        return pltpu.make_async_remote_copy(
            src_ref=part,
            dst_ref=part,
            send_sem=psend.at[g, ch],
            recv_sem=precv.at[g, ch],
            device_id=(other, z),
            device_id_type=MESH,
        )

    for ch in range(CHUNKS):
        own = z_ref.at[piece(ch)]
        late = ch == CHUNKS - 1

        @pl.when(z < (last - 1 if late else last))
        def _():
            hop(z, ch, 1, own).start()

        @pl.when(z > (1 if late else 0))
        def _():
            hop(z, ch, 0, own).start()

    for ch in range(CHUNKS):
        share(z, ch, z_ref.at[piece(ch)]).start()

    for i, bit in enumerate(bits[:-1]):
        pl.semaphore_signal(
            meet.at[i], inc=1, device_id=(across(bit) * PAIR + c, z), device_id_type=MESH
        )
        pl.semaphore_wait(meet.at[i], 1)

    z_load = pltpu.make_async_copy(z_ref, z_all.at[z, c], local_sem.at[0])
    z_load.start()
    f_load = pltpu.make_async_copy(f_ref, f_raw, local_sem.at[1])
    f_load.start()
    for load in loads:
        load.wait()

    lane = lax.broadcasted_iota(jnp.int32, (1, lanes), 1)
    owner = jnp.zeros_like(lane)
    for j in range(1, sites):
        owner = owner + jnp.where(lane >= j * held, 1, 0)
    local = lane - owner * held
    found = jnp.zeros(pos.shape, jnp.int32)
    for t in range(nz):
        found = jnp.where(pattern_ref[:, t : t + 1] == lane, t + 1, found)
    pos[...] = found
    for i in range(sites):
        line = pos[i * rows_here : i * rows_here + 1, :]
        for r in range(1, rows_here):
            at = i * rows_here + r
            line = jnp.maximum(line, pos[at : at + 1, :])
        need[i : i + 1, :] = jnp.where(line > 0, 1, 0)
    wanted = need[...]
    before = jnp.zeros_like(wanted)
    for d in range(1, held):
        before = before + jnp.where(local >= d, pltpu.roll(wanted, d, 1), 0)
    ranks[...] = before

    half_rows = tables.shape[0] // 2
    column = lax.broadcasted_iota(jnp.int32, (half_rows, tables.shape[1]), 1)
    gathered[...] = jnp.zeros_like(gathered)
    for r in range(rows_here):
        gathered[0, r : r + 1, :] = pos[pl.ds(k * rows_here + r, 1), :]
    for i in range(chips):
        gathered[1, i : i + 1, :] = need[pl.ds(i * PAIR + c, 1), :]
        gathered[2, i : i + 1, :] = ranks[pl.ds(i * PAIR + c, 1), :]
    own_slot = owner * MAX_COLUMN_BLOCKS + ranks[pl.ds(k, 1), :]
    own_slot = jnp.where(need[pl.ds(k, 1), :] > 0, own_slot, -1)
    places = jnp.zeros(column.shape, jnp.int32)
    positions = gathered[0]
    for t in range(slots):
        at = jnp.sum(jnp.where(own_slot == t, positions, 0), axis=1, keepdims=True)
        places = jnp.where(column == t, at, places)
    tables[0:half_rows, :] = places - 1
    blocks = jnp.zeros(column.shape, jnp.int32)
    needs, orders = gathered[1], gathered[2]
    first = q * PAIR * held
    for half in range(PAIR):
        mine = jnp.where(owner == q * PAIR + half, needs, 0)
        for j in range(MAX_COLUMN_BLOCKS):
            hit = jnp.where(orders == j, mine, 0)
            at = jnp.sum(hit * (lane - first), axis=1, keepdims=True)
            blocks = jnp.where(column == half * MAX_COLUMN_BLOCKS + j, at, blocks)
    tables[half_rows:, :] = blocks
    t_load = pltpu.make_async_copy(tables, scalars, local_sem.at[2])
    t_load.start()

    narrow = capacity_ref.shape[1]
    narrow_lane = lax.broadcasted_iota(jnp.int32, (8, narrow), 1)
    offset = z * height

    def rows_of(ref, base):
        parts = []
        for start in range(0, rows, narrow):
            part = None
            for r in range(start // height, min((start + narrow) // height, rows_here)):
                line = ref[pl.ds(base + r * blk // narrow + offset // narrow, 1), :]
                line = jnp.broadcast_to(line, narrow_lane.shape)
                shift = (r * height - start + narrow - offset % narrow) % narrow
                line = pltpu.roll(line, shift, 1)
                if part is None:
                    part = line
                else:
                    part = jnp.where(narrow_lane >= r * height - start, line, part)
            parts.append(part[0:1])
        return jnp.concatenate(parts, axis=1) if len(parts) > 1 else parts[0]

    scale_ref[...] = rows_of(capacity_ref, 0)
    spread_ref[...] = rows_of(spreads_ref, 0)
    maps = rows_of(buses_ref, k * (rows_here * blk // narrow))
    bus_ids = lax.broadcasted_iota(jnp.int32, onehot.shape, 0)
    onehot[...] = jnp.where(bus_ids == maps, 1.0, 0.0).astype(onehot.dtype)
    t_load.wait()

    def relay(g, ch):
        came_in(g, ch).wait_recv()

        @pl.when(jnp.logical_and(g < z, z < last))
        def _():
            hop(g, ch, 1).start()

        @pl.when(jnp.logical_and(g > z, z > 0))
        def _():
            hop(g, ch, 0).start()

        share(g, ch).start()

    def arrivals(d, ch):
        @pl.when(z - d >= 0)
        def _():
            relay(z - d, ch)

        @pl.when(z + d <= last)
        def _():
            relay(z + d, ch)

        if ch == CHUNKS - 1:
            own = z_ref.at[piece(ch)]

            @pl.when(jnp.logical_and(d == last - 1, z == 1))
            def _():
                hop(z, ch, 0, own).start()

            @pl.when(jnp.logical_and(d == last - 1, z == last - 1))
            def _():
                hop(z, ch, 1, own).start()

    def f_copy(target, source):
        return pltpu.make_async_remote_copy(
            src_ref=f_sorted.at[target],
            dst_ref=f_all.at[source],
            send_sem=fsend.at[target],
            recv_sem=frecv.at[source],
            device_id=(target * PAIR + c, z),
            device_id_type=MESH,
        )

    f_load.wait()

    def sort_for(target, store):
        def one(s, carry):
            blocks = []
            for r in range(rows_here):
                t = scalars[r, target * each + s]
                block = f_raw[r, jnp.maximum(t, 0)]
                if slots > nz:
                    block = jnp.where(t >= 0, block, jnp.zeros_like(block))
                blocks.append(block)
            store(s, jnp.concatenate(blocks, axis=0).T)
            return carry

        lax.fori_loop(0, each, one, 0)

    for e in range(1, chips):
        target = peer(e)

        def to_send(s, tile):
            f_sorted[target, s] = tile

        sort_for(target, to_send)
        f_copy(target, q).start()

    def to_own(s, tile):
        f_all[q, s] = tile

    sort_for(q, to_own)

    z_load.wait()

    for ch in range(CHUNKS - 1):
        arrivals(1, ch)

    @pl.when(jnp.logical_and(z > 0, z < last))
    def _():
        arrivals(1, CHUNKS - 1)

    arrivals(2, 0)
    for e in range(1, chips):
        f_copy(q, peer(e)).wait_recv()

    fewer = jnp.minimum(z, last - z)
    more = jnp.where(z < last - z, 1, -1)

    def group_at(p):
        late = jnp.logical_and(jnp.logical_and(z > 0, z < last), p >= last - 1)
        p = jnp.where(late, 2 * last - 1 - p, p)
        near = jnp.where(p % 2 == 1, -more, more) * ((p + 1) // 2)
        far = more * (p - fewer)
        return z + jnp.where(p <= 2 * fewer, near, far)

    def s_copy(g, ch, slot, target, source):
        size = bounds[ch + 1] - bounds[ch]
        return pltpu.make_async_remote_copy(
            src_ref=s_send.at[slot, target, pl.ds(0, size)],
            dst_ref=s_all.at[g, ch, source, pl.ds(0, size)],
            send_sem=ssend.at[slot, target],
            recv_sem=srecv.at[g, ch, source],
            device_id=(target * PAIR + c, z),
            device_id_type=MESH,
        )

    def b_copy(g, s, target, source):
        return pltpu.make_async_remote_copy(
            src_ref=b_send.at[s, target],
            dst_ref=b_all.at[g, s, source],
            send_sem=bsend.at[s, target],
            recv_sem=brecv.at[g, s, source],
            device_id=(target, z),
            device_id_type=MESH,
        )

    def seat(e):
        return flip(k, sites - e, sites)

    def c_copy(g, s, source):
        return pltpu.make_async_remote_copy(
            src_ref=c_send.at[g, s],
            dst_ref=c_all.at[s, source],
            send_sem=csend.at[g, s],
            recv_sem=crecv.at[s, source],
            device_id=(k, g),
            device_id_type=MESH,
        )

    beside = (1, last - 1)

    def is_end(plane):
        return jnp.logical_or(plane == 0, plane == last)

    def inner(plane):
        return jnp.logical_and(plane > 0, plane < last)

    def m_copy(end, s, source):
        return pltpu.make_async_remote_copy(
            src_ref=c_send.at[end * last, s],
            dst_ref=c_mid.at[end, s, source],
            send_sem=csend.at[end * last, s],
            recv_sem=mrecv.at[end, s, source],
            device_id=(k, beside[end]),
            device_id_type=MESH,
        )

    side = lax.broadcasted_iota(jnp.int32, (packed_rows, shared), 1) // share_of

    def pack(block, core):
        top, bottom = block[:packed_rows], block[hours - packed_rows :]
        if core:
            top = pltpu.roll(top, share_of, 1)
        else:
            bottom = pltpu.roll(bottom, share_of, 1)
        return jnp.where(side == 0, top, bottom)

    def multiply(g, ch, slot, kept):
        size = bounds[ch + 1] - bounds[ch]
        shared_in(g, ch).wait_recv()
        for half in range(PAIR):
            for b in range(held):
                z_work[half * held + b, 0:size, :] = z_all[
                    g, half, piece(ch), b * blk : (b + 1) * blk
                ]

        def product(i):
            total = None
            for s in range(each):
                term = lax.dot_general(
                    z_work[scalars[half_rows + i, s], 0:size, :],
                    f_all[i, s],
                    (((1,), (0,)), ((), ())),
                    preferred_element_type=jnp.float32,
                )
                total = term if total is None else total + term
            return total

        def one(e, carry):
            target = peer(e)
            s_send[slot, target, 0:size, :] = product(target).astype(s_send.dtype)
            s_copy(g, ch, slot, target, q).start()
            return carry

        lax.fori_loop(1, chips, one, 0)
        s_own[kept, 0:size, :] = product(q)

    def lane_of(p):
        return jnp.where(p == 1, 1, 0)

    def finish(p, ch, spare=False):
        g = group_at(p)
        size = bounds[ch + 1] - bounds[ch]
        total = s_own[CHUNKS if spare else ch, 0:size, :]
        for e in range(1, chips):
            s_copy(g, ch, 0, q, peer(e)).wait_recv()
            total = total + s_all[g, ch, peer(e), 0:size, :].astype(jnp.float32)
        s_sum[lane_of(p), bounds[ch] : bounds[ch + 1], :] = total
        for s in range(scens):
            if not bounds[ch] < (s + 1) * hours <= bounds[ch + 1]:
                continue
            spatial = s_sum[lane_of(p), s * hours : (s + 1) * hours, :].astype(jnp.bfloat16)
            weather = jnp.dot(temporal_ref[...], spatial, preferred_element_type=jnp.float32)
            spread = spread_ref[...]
            values = scale_ref[...] * jnp.exp(spread * weather - 0.5 * spread * spread)
            sums = lax.dot_general(
                values.astype(jnp.bfloat16),
                onehot[...],
                (((1,), (1,)), ((), ())),
                preferred_element_type=jnp.float32,
            )

            @pl.when(p > 0)
            def _():
                for e in range(1, sites):
                    b_copy(g, s, seat(e), k).wait_send()

            for i in range(chips):
                block = sums[:, i * shared : (i + 1) * shared]
                for core in range(PAIR):
                    b_send[s, i * PAIR + core] = pack(block, core).astype(b_send.dtype)
            for e in range(1, sites):
                b_copy(g, s, seat(e), k).start()
            b_all[g, s, k] = b_send[s, k]

    def forward(p, s):
        g = group_at(p)
        for e in range(1, sites):
            b_copy(g, s, k, seat(e)).wait_recv()
        total = b_all[g, s, 0].astype(jnp.float32)
        for i in range(1, sites):
            total = total + b_all[g, s, i].astype(jnp.float32)

        @pl.when(p == 0)
        def _():
            c_all[s, z] = total

        @pl.when(p > 0)
        def _():
            c_send[g, s] = total

            @pl.when(jnp.logical_or(is_end(z), inner(g)))
            def _():
                c_copy(g, s, z).start()

            for end, near in enumerate(beside):

                @pl.when(jnp.logical_and(inner(z), jnp.logical_and(g == end * last, z != near)))
                def _():
                    m_copy(end, s, z).start()

    def free(g, ch, slot):
        for e in range(1, chips):
            s_copy(g, ch, slot, peer(e), q).wait_send()

    def done_in(s):
        return next(ch for ch in range(CHUNKS) if (s + 1) * hours <= bounds[ch + 1])

    final = CHUNKS - 1

    def stage(p, ch, spare=False):
        g = group_at(p)

        @pl.when(p > 0)
        def _():
            free(g, ch, ch)

        multiply(g, ch, ch, CHUNKS if spare else ch)

    def position(p, carry):
        for ch in range(CHUNKS):
            if ch == final:

                @pl.when(jnp.logical_or(p != 1, inner(z)))
                def _():
                    stage(p, ch)

            else:
                stage(p, ch)
            for s in range(scens):
                at = done_in(s) + 3
                if at % CHUNKS == ch:
                    back = at // CHUNKS
                    ready = p >= back
                    if done_in(s) == final:
                        natural = jnp.logical_or(p != 1 + back, inner(z))
                        ready = jnp.logical_and(ready, natural)

                    @pl.when(ready)
                    def _():
                        forward(p - back, s)

            if ch > 0:
                finish(p, ch - 1)
            else:

                @pl.when(jnp.logical_and(p > 0, jnp.logical_or(p != 2, inner(z))))
                def _():
                    finish(p - 1, final)

            step = ch + 1
            if step < CHUNKS:

                @pl.when(p > 2)
                def _():
                    arrivals(p, step)
            else:

                @pl.when(jnp.logical_and(p >= 2, p < last))
                def _():
                    arrivals(p + 1, 0)

            for part in range(1, CHUNKS):
                if 2 * part % CHUNKS == ch:

                    @pl.when(p == 2 * part // CHUNKS)
                    def _():
                        arrivals(2, part)

        return carry

    lax.fori_loop(0, groups, position, 0)

    @pl.when(is_end(z))
    def _():
        arrivals(1, final)
        stage(1, final, True)

    finish(last, final)
    for s in range(scens):
        if done_in(s) < final and done_in(s) + 3 >= CHUNKS:
            forward(last, s)

    @pl.when(is_end(z))
    def _():
        finish(1, final, True)

    for s in range(scens):
        if done_in(s) == final:
            forward(last, s)

    @pl.when(is_end(z))
    def _():
        for s in range(scens):
            if done_in(s) == final:
                forward(1, s)

    for g in range(groups):
        for ch in range(CHUNKS):
            share(g, ch).wait_send()

            @pl.when(jnp.logical_and(g <= z, z < last))
            def _():
                hop(g, ch, 1).wait_send()

            @pl.when(jnp.logical_and(g >= z, z > 0))
            def _():
                hop(g, ch, 0).wait_send()

    for end, near in enumerate(beside):

        @pl.when(jnp.logical_and(inner(z), z == near))
        def _():
            for s in range(scens):
                total = c_send[end * last, s]
                for source in range(1, last):
                    if source != near:
                        m_copy(end, s, source).wait_recv()
                        total = total + c_mid[end, s, source]
                c_send[end * last, s] = total
                c_copy(end * last, s, z).start()

    def unpack(packed, s, ref):
        rest = pltpu.roll(packed[2 * packed_rows - hours :], share_of, 1)
        whole = jnp.concatenate([packed, rest], axis=0)
        ref[:, s * hours : (s + 1) * hours] = whole.T[:share_of]

    for s in range(scens):
        unpack(c_all[s, z], s, near_ref)
        c_sum[s] = jnp.zeros_like(c_sum[s])
    for s in range(scens):
        for d in range(1, groups):
            source = (z + d) % groups
            direct = jnp.logical_or(inner(z), is_end(source))
            for end, near in enumerate(beside):
                direct = jnp.logical_or(direct, jnp.logical_and(z == end * last, source == near))

            @pl.when(direct)
            def _():
                c_copy(z, s, source).wait_recv()
                c_sum[s] = c_sum[s] + c_all[s, source]

        unpack(c_sum[s], s, far_ref)

    for ch in range(CHUNKS):
        free(z, ch, ch)
    for e in range(1, chips):
        f_copy(peer(e), q).wait_send()
    for s in range(scens):
        for e in range(1, sites):
            b_copy(z, s, seat(e), k).wait_send()
    for s in range(scens):
        for d in range(1, groups):
            c_copy((z + d) % groups, s, z).wait_send()


def bounds_of(width):
    unit = width // 21
    return [0, 9 * unit, 18 * unit, width]


def shards(normals, pattern, factor, temporal, capacity, spread, bus_map, buses):
    sites = lax.axis_size("site")
    groups = lax.axis_size("scen")
    depth, width = normals.shape
    rows_here, nz, height, blk = factor.shape
    hours = temporal.shape[0]
    scens = width // hours
    chips = sites // PAIR
    bounds = bounds_of(width)
    step = max(b - a for a, b in zip(bounds, bounds[1:]))
    slots = sites * MAX_COLUMN_BLOCKS
    each = slots // chips
    rows = rows_here * height
    shared = buses // chips
    packed_rows = (hours // 2 + 7) // 8 * 8
    block_count = depth // blk
    lanes = -(-block_count * sites // LANES) * LANES
    half_rows = -(-max(chips, rows_here) // 8) * 8

    bf16, f32, i32 = jnp.bfloat16, jnp.float32, jnp.int32
    dma = pltpu.SemaphoreType.DMA
    whole = pl.BlockSpec(memory_space=pltpu.VMEM)
    anywhere = pl.BlockSpec(memory_space=pltpu.HBM)
    scratch = [
        pltpu.VMEM(pattern.shape, i32),
        pltpu.VMEM(temporal.shape, bf16),
        pltpu.VMEM((capacity.size // LANES, LANES), f32),
        pltpu.VMEM((spread.size // LANES, LANES), f32),
        pltpu.VMEM((bus_map.size // LANES, LANES), i32),
        pltpu.VMEM((groups, PAIR, width, depth), bf16),
        pltpu.VMEM((PAIR * block_count, step, blk), bf16),
        pltpu.VMEM((rows_here, nz, height, blk), bf16),
        pltpu.VMEM((chips, each, blk, rows), bf16),
        pltpu.VMEM((chips, each, blk, rows), bf16),
        pltpu.VMEM((CHUNKS, chips, step, rows), bf16),
        pltpu.VMEM((CHUNKS + 1, step, rows), f32),
        pltpu.VMEM((groups, CHUNKS, chips, step, rows), bf16),
        pltpu.VMEM((2, width, rows), f32),
        pltpu.VMEM((scens, sites, packed_rows, shared), bf16),
        pltpu.VMEM((groups, scens, sites, packed_rows, shared), bf16),
        pltpu.VMEM((groups, scens, packed_rows, shared), f32),
        pltpu.VMEM((scens, groups, packed_rows, shared), f32),
        pltpu.VMEM((2, scens, groups, packed_rows, shared), f32),
        pltpu.VMEM((scens, packed_rows, shared), f32),
        pltpu.VMEM((buses, rows), bf16),
        pltpu.VMEM((1, rows), f32),
        pltpu.VMEM((1, rows), f32),
        pltpu.VMEM((pattern.shape[0], lanes), i32),
        pltpu.VMEM((sites, lanes), i32),
        pltpu.VMEM((sites, lanes), i32),
        pltpu.VMEM((3, half_rows, lanes), i32),
        pltpu.VMEM((2 * half_rows, LANES), i32),
        pltpu.SMEM((2 * half_rows, LANES), i32),
        dma((8,)),
        dma((2, groups, CHUNKS)),
        dma((groups, CHUNKS)),
        dma((groups, CHUNKS)),
        dma((groups, CHUNKS)),
        dma((chips,)),
        dma((chips,)),
        dma((CHUNKS, chips)),
        dma((groups, CHUNKS, chips)),
        dma((scens, sites)),
        dma((groups, scens, sites)),
        dma((groups, scens)),
        dma((scens, groups)),
        dma((2, scens, groups)),
        pltpu.SemaphoreType.REGULAR((max(chips.bit_length() - 2, 1),)),
    ]
    taken = sum(
        math.prod(ref.shape) * ref.dtype.itemsize
        for ref in scratch
        if ref.memory_space == pltpu.VMEM
    )
    limit = min(taken + taken // 16 + VMEM_MARGIN, VMEM_LIMIT)
    near, far = pl.pallas_call(
        functools.partial(kernel, chips, groups, slots, hours),
        out_shape=[jax.ShapeDtypeStruct((buses // sites, width), f32)] * 2,
        in_specs=[anywhere] * 7,
        out_specs=[whole] * 2,
        scratch_shapes=scratch,
        compiler_params=pltpu.CompilerParams(
            collective_id=0, has_side_effects=True, vmem_limit_bytes=limit
        ),
    )(
        *(
            pltpu.with_memory_space_constraint(x, pltpu.HBM)
            for x in (
                pattern,
                normals.T,
                factor,
                temporal,
                capacity.reshape(-1, LANES),
                spread.reshape(-1, LANES),
                bus_map.reshape(-1, LANES),
            )
        )
    )
    return near + far


def solution(mesh):
    placed = (P("site", "scen"), P(), P("site", None, "scen", None), P(), P("site"), P("site"), P())
    sites = mesh.shape["site"]

    def whole(normals, pattern, factor, temporal, capacity, spread, bus_map):
        buses = factor.shape[0] * factor.shape[3] // 16

        def body(*args):
            return shards(*args, buses)

        return jax.shard_map(
            body, mesh=mesh, in_specs=placed, out_specs=P("site", "scen"), check_vma=False
        )(normals, pattern, factor, temporal, capacity, spread, bus_map)

    return whole
```
